512 devices in a mesh: ctx: 64 (over y, x, z_lo), fsdp: 8 (over z_hi, core).
Axes of the slice: x: 4, y: 8, z: 8 (z_hi: 4, z_lo: 2; z = z_hi * 2 + z_lo), core: 2. Of those that a mesh axis runs over, the one named last changes fastest.
Arguments:
- rotated_query_rows: bfloat16 [12288, 4096], P('ctx', 'fsdp'), may hold values from -6 to 6
- rotated_key_rows: bfloat16 [12288, 4096], P('ctx', 'fsdp'), may hold values from -6 to 6
- saved_value_rows: bfloat16 [12288, 4096], P('ctx', 'fsdp'), may hold values from -6 to 6
- projection_output_gradient: bfloat16 [12288, 5120], P('ctx', 'fsdp'), may hold values from -6 to 6
- frozen_weight_codes: int32 [5120, 4096], P('ctx', 'fsdp'), may hold values from 0 to 15
- block_scale_index: int32 [5120, 64], P('ctx', 'fsdp'), may hold values from 0 to 255
- block_scale_table: float32 [256], replicated, may hold values from 0.008385255 to 0.08385255
- adapter_down_matrix: bfloat16 [64, 4096], P('ctx', 'fsdp'), may hold values from -0.75 to 0.75
- adapter_up_matrix: bfloat16 [64, 5120], P('ctx', 'fsdp'), may hold values from -0.078125 to 0.078125
Outputs:
- query_grad: bfloat16 [12288, 4096], P('ctx', 'fsdp')
- key_grad: bfloat16 [12288, 4096], P('ctx', 'fsdp')
- value_grad: bfloat16 [12288, 4096], P('ctx', 'fsdp')
- down_matrix_gradient: float32 [64, 4096], P('ctx', 'fsdp')
- up_matrix_gradient: float32 [64, 5120], P('ctx', 'fsdp')
The draws below stay inside these ranges and needn't reach their ends.
All inputs are finite; a program needn't handle non-finite values.
Results may differ from the reference program's by a relative error of at most 0.0093.
Values may be sent and summed in bfloat16 or wider, within the bound.
A program may use at most 64 MiB of HBM per device.

```python
import math
import jax
import jax.numpy as jnp
from jax import lax

MODEL_WIDTH = 5120
HEAD_WIDTH = 128
HPD = 4
ADAPTER_RANK = 64
QBLOCK = 64
LEVELS = 256
ATTENTION_HEADS = 32
SEQ = 12288
GROUP = 1536
SHIFT = 768


def drawn_pair(key):
    base_key = jax.random.fold_in(key, 7)
    query_key, key_key = jax.random.split(base_key, 2)
    full_shape = (SEQ, ATTENTION_HEADS * HEAD_WIDTH)
    query_base = 1.6 * jax.random.truncated_normal(query_key, -3.75, 3.75, full_shape, jnp.float32)
    key_base = 1.6 * jax.random.truncated_normal(key_key, -3.75, 3.75, full_shape, jnp.float32)
    return (query_base, key_base)


def draw_rotated_query_rows(key, part):
    return drawn_pair(key)[0].astype(jnp.bfloat16)


def draw_rotated_key_rows(key, part):
    return drawn_pair(key)[1].astype(jnp.bfloat16)


def place_ends(drawn, own_key, smallest, largest):
    extent = drawn.shape
    index_at = [jax.random.randint(jax.random.fold_in(own_key, axis), (), 0, extent[axis]) for axis in range(len(extent))]
    drawn = drawn.at[tuple(index_at)].set(smallest)
    longest = extent.index(max(extent))
    index_at[longest] = (index_at[longest] + 1) % extent[longest]
    return drawn.at[tuple(index_at)].set(largest)


def levels(stream_key, dims, cuts, least, top_value):
    def one(position, blocks):
        heights = jax.random.uniform(jax.random.fold_in(jax.random.fold_in(stream_key, 6), position), (blocks,), jnp.float32, least / len(cuts), top_value / len(cuts))
        return jnp.repeat(jnp.exp(heights), dims[position] // blocks).reshape((-1,) + (1,) * (len(dims) - position - 1))

    level = one(*cuts[0])
    for cut in cuts[1:]:
        level = level * one(*cut)
    return level


def bell_draw(rng, dims, spread, limit, shards=(), held_as=jnp.bfloat16):
    entries = spread * jax.random.normal(rng, dims, jnp.float32)
    if shards:
        entries = entries * levels(rng, dims, shards, -0.22, 0.18)
    return jnp.clip(entries, -limit, limit).astype(held_as)


def setup_inputs(seed: int = 0) -> dict:
    splits = jax.random.split(jax.random.key(seed), 10)
    rotated_query_rows = draw_rotated_query_rows(jax.random.fold_in(splits[9], 71), 0)
    rotated_key_rows = draw_rotated_key_rows(jax.random.fold_in(splits[9], 71), 0)
    saved_value_rows = bell_draw(splits[2], (SEQ, ATTENTION_HEADS * HEAD_WIDTH), 1.0, 6.0, ((0, 64), (1, 8)))
    projection_output_gradient = bell_draw(splits[3], (SEQ, MODEL_WIDTH), 1.0, 6.0, ((0, 64), (1, 8)))
    frozen_weight_codes = place_ends(jax.random.randint(splits[4], (MODEL_WIDTH, ATTENTION_HEADS * HEAD_WIDTH), 0, 16), jax.random.fold_in(splits[4], 1), 0, 15).astype(jnp.int32)
    block_scale_index = place_ends(jax.random.randint(splits[5], (MODEL_WIDTH, ATTENTION_HEADS * HEAD_WIDTH // QBLOCK), 0, LEVELS), jax.random.fold_in(splits[5], 1), 0, LEVELS - 1).astype(jnp.int32)
    block_scale_table = jnp.clip(jnp.exp(jax.random.uniform(splits[6], (LEVELS,), jnp.float32, math.log(0.008385255), math.log(0.08385255))), 0.008385255, 0.08385255)
    adapter_down_matrix = bell_draw(splits[7], (ADAPTER_RANK, ATTENTION_HEADS * HEAD_WIDTH), ADAPTER_RANK ** -0.5, 0.75, ((0, 64), (1, 8)))
    adapter_up_matrix = bell_draw(splits[8], (ADAPTER_RANK, MODEL_WIDTH), MODEL_WIDTH ** -0.5, 0.078125, ((0, 64), (1, 8)))
    return dict(rotated_query_rows=rotated_query_rows, rotated_key_rows=rotated_key_rows, saved_value_rows=saved_value_rows, projection_output_gradient=projection_output_gradient, frozen_weight_codes=frozen_weight_codes, block_scale_index=block_scale_index, block_scale_table=block_scale_table, adapter_down_matrix=adapter_down_matrix, adapter_up_matrix=adapter_up_matrix)


nf4_values = (-1.0, -0.6961928009986877, -0.5250730514526367, -0.39491748809814453, -0.28444138169288635, -0.18477343022823334, -0.09105003625154495, 0.0, 0.07958029955625534, 0.16093020141124725, 0.24611230194568634, 0.33791524171829224, 0.44070982933044434, 0.5626170039176941, 0.7229568362236023, 1.0)
adapter_scale = 0.25
masked = -1.0e30


def dequantize(frozen_weight_codes, block_scale_index, block_scale_table):
    table = jnp.asarray(nf4_values, dtype=jnp.float32)
    values = table[frozen_weight_codes]
    scales = jnp.repeat(block_scale_table[block_scale_index], QBLOCK, axis=1)
    return (values * scales).astype(jnp.bfloat16)


def attend_one(blocks_in):
    query_blk, key_blk, value_blk, grad_blk = blocks_in
    group_len = query_blk.shape[0]
    score_scale = HEAD_WIDTH ** -0.5
    scores = jnp.dot(query_blk, key_blk.T, preferred_element_type=jnp.float32) * score_scale
    row_iota = lax.broadcasted_iota(jnp.int32, (group_len, group_len), 0)
    col_iota = lax.broadcasted_iota(jnp.int32, (group_len, group_len), 1)
    scores = jnp.where(col_iota <= row_iota, scores, masked)
    row_max = jnp.max(scores, axis=-1, keepdims=True)
    row_sum = jnp.sum(jnp.exp(scores - row_max), axis=-1, keepdims=True)
    log_norm = row_max + jnp.log(row_sum)
    prob_full = jnp.exp(scores - log_norm)
    prob_half = prob_full.astype(jnp.bfloat16)
    attention_output = jnp.dot(prob_half, value_blk, preferred_element_type=jnp.float32).astype(jnp.bfloat16)
    prob_grad = jnp.dot(grad_blk, value_blk.T, preferred_element_type=jnp.float32)
    row_delta = jnp.sum(prob_full * prob_grad, axis=-1, keepdims=True)
    score_grad = (prob_full * (prob_grad - row_delta) * score_scale).astype(jnp.bfloat16)
    query_grad = jnp.dot(score_grad, key_blk, preferred_element_type=jnp.float32)
    key_grad = jnp.dot(score_grad.T, query_blk, preferred_element_type=jnp.float32)
    value_grad = jnp.dot(prob_half.T, grad_blk, preferred_element_type=jnp.float32)
    return query_grad, key_grad, value_grad, attention_output


def reference(rotated_query_rows, rotated_key_rows, saved_value_rows, projection_output_gradient, frozen_weight_codes, block_scale_index, block_scale_table, adapter_down_matrix, adapter_up_matrix):
    decoded_weight = dequantize(frozen_weight_codes, block_scale_index, block_scale_table)
    adapter_backward = (adapter_scale * jnp.dot(projection_output_gradient, adapter_up_matrix.T, preferred_element_type=jnp.float32)).astype(jnp.bfloat16)
    attention_gradient = (jnp.dot(projection_output_gradient, decoded_weight, preferred_element_type=jnp.float32) + jnp.dot(adapter_backward, adapter_down_matrix, preferred_element_type=jnp.float32)).astype(jnp.bfloat16)
    seq_len = rotated_query_rows.shape[0]
    head_ids = jnp.arange(ATTENTION_HEADS)
    shifted = (head_ids % HPD) >= HPD // 2

    def arrange(tensor):
        tensor = tensor.reshape(seq_len, ATTENTION_HEADS, HEAD_WIDTH)
        tensor = jnp.where(shifted[None, :, None], jnp.roll(tensor, -SHIFT, axis=0), tensor)
        tensor = tensor.reshape(seq_len // GROUP, GROUP, ATTENTION_HEADS, HEAD_WIDTH).transpose(0, 2, 1, 3)
        return tensor.reshape(-1, GROUP, HEAD_WIDTH)

    def restore(tensor):
        tensor = tensor.reshape(seq_len // GROUP, ATTENTION_HEADS, GROUP, HEAD_WIDTH).transpose(0, 2, 1, 3)
        tensor = tensor.reshape(seq_len, ATTENTION_HEADS, HEAD_WIDTH)
        tensor = jnp.where(shifted[None, :, None], jnp.roll(tensor, SHIFT, axis=0), tensor)
        return tensor.reshape(seq_len, ATTENTION_HEADS * HEAD_WIDTH)

    results = lax.map(attend_one, (arrange(rotated_query_rows), arrange(rotated_key_rows), arrange(saved_value_rows), arrange(attention_gradient)))
    query_grad = restore(results[0]).astype(jnp.bfloat16)
    key_grad = restore(results[1]).astype(jnp.bfloat16)
    value_grad = restore(results[2]).astype(jnp.bfloat16)
    attention_output = restore(results[3])
    adapter_middle = jnp.dot(attention_output, adapter_down_matrix.T, preferred_element_type=jnp.float32).astype(jnp.bfloat16)
    up_matrix_gradient = adapter_scale * jnp.dot(adapter_middle.T, projection_output_gradient, preferred_element_type=jnp.float32)
    down_matrix_gradient = jnp.dot(adapter_backward.T, attention_output, preferred_element_type=jnp.float32)
    return (query_grad, key_grad, value_grad, down_matrix_gradient, up_matrix_gradient)
```

```python
import jax
import jax.numpy as jnp
from jax import lax
from jax.experimental import pallas as pl
from jax.experimental.pallas import tpu as pltpu
from jax.sharding import PartitionSpec as P

HEAD_WIDTH = 128
MESH = pl.DeviceIdType.MESH
BLOCK = 384
nf4_values = (
    -1.0,
    -0.6961928009986877,
    -0.5250730514526367,
    -0.39491748809814453,
    -0.28444138169288635,
    -0.18477343022823334,
    -0.09105003625154495,
    0.0,
    0.07958029955625534,
    0.16093020141124725,
    0.24611230194568634,
    0.33791524171829224,
    0.44070982933044434,
    0.5626170039176941,
    0.7229568362236023,
    1.0,
)
adapter_scale = 0.25
masked = -1e30
f32, bf16 = jnp.float32, jnp.bfloat16
SEMS = 256


def dequantize(frozen_weight_codes, block_scale_index, block_scale_table):
    values = jnp.zeros(frozen_weight_codes.shape, f32)
    for level_code in range(16):
        values = values + jnp.where(frozen_weight_codes == level_code, nf4_values[level_code], 0.0)
    level_iota = lax.broadcasted_iota(jnp.int32, (1, 1, block_scale_table.shape[0]), 2)
    picked = jnp.sum(
        jnp.where(block_scale_index[:, :, None] == level_iota, block_scale_table, 0.0), axis=-1
    )
    scales = jnp.repeat(picked, frozen_weight_codes.shape[1] // block_scale_index.shape[1], axis=1)
    return (values * scales).astype(bf16)


def nt(a, b):
    return lax.dot_general(a, b, (((1,), (1,)), ((), ())), preferred_element_type=f32)


def tn(a, b):
    return lax.dot_general(a, b, (((0,), (0,)), ((), ())), preferred_element_type=f32)


def nn(a, b):
    return jnp.dot(a, b, preferred_element_type=f32)


def kernel(
    q_ref, k_ref, v_ref, g_ref, w_ref, ad_ref, au_ref,
    dq_ref, dk_ref, dv_ref, dn_ref, up_ref,
    WA, WB, GB, QU, KU, VU, DU, PT, KT, OB, OS, DQS, DKS, DVS, DKA, DVA, DOB,
    AD1, AD2, PSS, PSR, PSG, UPD, R1, S2, R2, ss, rs, ls,
):
    ctx = lax.axis_index("ctx")
    f = lax.axis_index("fsdp")
    y, g = ctx // 8, ctx % 8
    x, zl = g // 2, g % 2
    c = f % 2
    partner = f + 1 - 2 * c
    scale = HEAD_WIDTH ** (-0.5)
    is_host = (x % 2) == c
    unit_head = 2 * (x // 2) + zl

    counter = [0]
    sends = []

    def ids(n):
        first = counter[0]
        counter[0] += n
        return first

    def remote(src, dst, sem, to_ctx, to_f, recv=None):
        return pltpu.make_async_remote_copy(
            src_ref=src,
            dst_ref=dst,
            send_sem=ss.at[sem],
            recv_sem=rs.at[sem if recv is None else recv],
            device_id={"ctx": to_ctx, "fsdp": to_f},
            device_id_type=MESH,
        )

    def go(src, dst, sem, to_ctx, to_f):
        copy = remote(src, dst, sem, to_ctx, to_f)
        copy.start()
        sends.append(copy)
        return copy

    def arrived(dst, sem):
        pltpu.make_async_copy(dst, dst, rs.at[sem]).wait()

    def row(dy):
        return (y + dy) % 8

    def at(yy, gg):
        return yy * 8 + gg

    def ydev(dy):
        return at(row(dy), g)

    def xdev(dx):
        return at(y, ((x + dx) % 4) * 2 + zl)

    def fdev(df):
        return (f + df) % 8

    other_row = jnp.where(x < 2, (y + 7) % 8, (y + 1) % 8)
    other_g = jnp.where(x < 2, 4, 0)

    barrier = pltpu.get_barrier_semaphore()
    peers = [(at(y, (g + j) % 8), f) for j in range(1, 8)]
    peers += [(ydev(j), f) for j in range(1, 8)]
    peers += [(ctx, fdev(j)) for j in range(1, 8)]
    peers += [(at(other_row, other_g + j), f) for j in range(4)]
    for to_ctx, to_f in peers:
        pl.semaphore_signal(
            barrier, inc=1, device_id={"ctx": to_ctx, "fsdp": to_f}, device_id_type=MESH
        )
    pl.semaphore_wait(barrier, len(peers))

    pair = ctx + 1 - 2 * zl
    i = ids(2)
    wl, wr = w_ref.at[:, 0:256], w_ref.at[:, 256:512]
    s1 = [go(wl, WA.at[y, g], i, pair, f), go(wr, WB.at[y, g], i + 1, pair, f)]
    own_copies = [
        pltpu.make_async_copy(wl, WA.at[y, g], ls.at[0]),
        pltpu.make_async_copy(wr, WB.at[y, g], ls.at[1]),
        pltpu.make_async_copy(g_ref, GB.at[f], ls.at[2]),
    ]
    for copy in own_copies:
        copy.start()

    gi = ids(11)
    half = [pl.ds(0, 96), pl.ds(96, 96)]
    go(g_ref, GB.at[f], gi, ctx, partner)
    go(g_ref, GB.at[f], gi + 1, ctx, fdev(2))
    go(g_ref, GB.at[f], gi + 2, ctx, fdev(6))

    AD1[g] = jnp.concatenate([ad_ref[...].astype(f32), au_ref[...].astype(f32)], axis=1)
    ai = ids(8)
    for j in range(1, 8):
        go(AD1.at[g], AD1.at[g], ai + j, at(y, (g + j) % 8), f)

    def slab_of(head):
        if head < 2:
            return y, g
        return jnp.where(x < 2, (y + 7) % 8, y), (g + 4) % 8

    def host_of(head):
        yy, _ = slab_of(head)
        return at(yy, (2 * (head // 2) + c) * 2 + head % 2)

    conditional = []

    def to_hosts(src_ref, dst_buf, recv_base):
        send_base = ids(4)
        for head in range(4):
            dest = host_of(head)
            _, slot = slab_of(head)
            src = src_ref.at[:, head * 128 : (head + 1) * 128]
            dst = dst_buf.at[slot]
            away = dest != ctx
            copy = remote(src, dst, send_base + head, dest, f, recv_base + slot)

            @pl.when(away)
            def _():
                copy.start()

            @pl.when(jnp.logical_not(away))
            def _():
                pltpu.make_async_copy(src, dst, rs.at[recv_base + slot]).start()

            conditional.append((away, copy))

    ki, qi, vi, di = ids(8), ids(8), ids(8), ids(8)
    to_hosts(k_ref, KU, ki)
    to_hosts(q_ref, QU, qi)
    to_hosts(v_ref, VU, vi)

    for copy in own_copies:
        copy.wait()
    for copy in s1:
        copy.wait_recv()

    def PB(dy, dx):
        return WB.at[row(dy), pl.ds(((x + dx) % 4) * 2, 2)]

    def QA(dy, h):
        return WA.at[row(dy), pl.ds(4 * h, 4)]

    yb = {d: ids(1) for d in (-4, -3, -2, -1, 1, 2, 3)}
    xb = {(s, d): ids(1) for s in (-1, 1) for d in range(-4, 4)}
    xr = {d: ids(1) for d in range(-4, 4)}
    up_relay = (-2, -1, 0, 1)

    def b_to_x(d):
        go(PB(d, 0), PB(d, 0), xb[(-1, d)], xdev(1), f)
        go(PB(d, 0), PB(d, 0), xb[(1, d)], xdev(-1), f)

    def b_up(d):
        go(PB(d, 0), PB(d, 0), yb[d - 1], ydev(1), f)

    def b_down(d):
        go(PB(d, 0), PB(d, 0), yb[d + 1], ydev(-1), f)

    def b_arrived(d):
        arrived(PB(d, 0), yb[d])

    def x_relay(d):
        side = -1 if d in up_relay else 1
        arrived(PB(d, side), xb[(side, d)])
        go(PB(d, side), PB(d, side), xr[d], xdev(-side), f)

    b_up(0)
    b_down(0)
    mine = WA.at[y, pl.ds(x * 2, 2)]
    xa = ids(3)
    go(mine, mine, xa, xdev(1), f)
    go(mine, mine, xa + 1, xdev(-1), f)
    go(mine, mine, xa + 2, xdev(2), f)
    b_to_x(0)

    for j in range(1, 8):
        arrived(AD1.at[(g + 8 - j) % 8], ai + j)
    AD2[y] = jnp.concatenate([AD1[j] for j in range(8)], axis=0)
    bi = ids(8)
    for j in range(1, 8):
        go(AD2.at[y], AD2.at[y], bi + j, ydev(j), f)

    for k, dx in enumerate((-1, 1, 2)):
        block = WA.at[y, pl.ds(((x + dx) % 4) * 2, 2)]
        arrived(block, xa + k)

    ya = {(d, h): ids(1) for d in (-4, -3, -2, -1, 1, 2, 3, 4) for h in (0, 1)}

    def a_up(d, h):
        go(QA(d, h), QA(d, h), ya[(d - 1, h)], ydev(1), f)

    def a_down(d, h):
        go(QA(d, h), QA(d, h), ya[(d + 1, h)], ydev(-1), f)

    def a_arrived(d, h):
        arrived(QA(d, h), ya[(d, h)])

    for h in (0, 1):
        a_up(0, h)
        a_down(0, h)

    def b_step(d):
        b_arrived(-d)
        b_up(-d)
        b_to_x(-d)
        b_arrived(d)
        if d < 3:
            b_down(d)
        b_to_x(d)

    b_step(1)
    x_relay(0)

    below, above, across = fdev(6), fdev(2), fdev(4)
    arrived(GB.at[below], gi + 1)
    go(GB.at[below, half[0]], GB.at[below, half[0]], gi + 3, ctx, above)
    go(GB.at[below], GB.at[below], gi + 4, ctx, partner)
    arrived(GB.at[above], gi + 2)
    go(GB.at[above, half[1]], GB.at[above, half[1]], gi + 5, ctx, below)
    go(GB.at[above], GB.at[above], gi + 6, ctx, partner)

    b_step(2)
    x_relay(-1)
    x_relay(1)
    for h in (0, 1):
        a_arrived(-1, h)
        a_up(-1, h)
        a_arrived(1, h)
        a_down(1, h)

    def sum_start(n, piece):
        PSS[n] = piece.reshape(8, 24, 128)
        base = ids(8)
        for j in range(1, 8):
            to = fdev(j)
            go(PSS.at[n, to], PSR.at[n, f], base + j, ctx, to)
        return base

    def sum_middle(n, base, factor):
        total = PSS[n, f]
        for j in range(1, 8):
            frm = fdev(8 - j)
            arrived(PSR.at[n, frm], base + j)
            total = total + PSR[n, frm]
        PSG[n, f] = (total * factor).astype(bf16).astype(f32)
        base = ids(8)
        for j in range(1, 8):
            go(PSG.at[n, f], PSG.at[n, f], base + j, ctx, fdev(j))
        return base

    def sum_end(n, base):
        for j in range(1, 8):
            arrived(PSG.at[n, fdev(8 - j)], base + j)
        return PSG[n].reshape(192, 128).astype(bf16)

    for j in range(1, 8):
        arrived(AD2.at[row(8 - j)], bi + j)
    adapters = AD2[...].reshape(64, 1152).astype(bf16)
    adapters = jnp.concatenate([adapters, jnp.zeros_like(adapters)], axis=0)
    down_full, up_piece = adapters[:, :512], adapters[:, 512:]
    back_base = sum_start(0, nt(g_ref[...], up_piece))

    b_step(3)
    x_relay(-2)
    x_relay(2)

    oi = ids(4)
    oh = ids(8)

    def source_of(slot):
        if slot < 4:
            return jnp.where(x < 2, at(y, slot), at(y, slot + 4))
        return jnp.where(x < 2, at(y, slot), at(row(1), slot - 4))

    head_columns = pl.ds(pl.multiple_of(unit_head * 128, 128), 128)
    hosted = []

    def returned(buf, dst_ref, recv_base, send_sem, slot):
        dest = source_of(slot)
        src, dst = buf.at[slot], dst_ref.at[:, head_columns]
        copy = remote(src, dst, send_sem, dest, f, recv_base + unit_head)
        return dest != ctx, copy, src, dst

    def from_host(*what):
        away, copy, src, dst = returned(*what)
        recv_base = what[2]

        @pl.when(away)
        def _():
            copy.start()

        @pl.when(jnp.logical_not(away))
        def _():
            pltpu.make_async_copy(src, dst, rs.at[recv_base + unit_head]).start()

        hosted.append(what)

    blocks = 8 // (BLOCK // 192)

    def two(buf, b):
        return buf[2 * b : 2 * b + 2].reshape(BLOCK, 128)

    def tile(b, kb):
        return b * (b + 1) // 2 + kb

    @pl.when(is_host)
    def _():
        for s in range(8):
            arrived(KU.at[s], ki + s)
            arrived(QU.at[s], qi + s)
        key_at = lax.broadcasted_iota(jnp.int32, (BLOCK, BLOCK), 0)
        query_at = lax.broadcasted_iota(jnp.int32, (BLOCK, BLOCK), 1)
        seen = key_at <= query_at
        for s in range(8):
            arrived(VU.at[s], vi + s)
        for b in range(blocks):
            query = two(QU, b)
            parts = []
            for kb in range(b + 1):
                part = nt(two(KU, kb), query) * scale
                parts.append(jnp.where(seen, part, masked) if kb == b else part)
            top = jnp.max(parts[0], axis=0, keepdims=True)
            for part in parts[1:]:
                top = jnp.maximum(top, jnp.max(part, axis=0, keepdims=True))
            parts = [jnp.exp(part - top) for part in parts]
            total = jnp.sum(parts[0], axis=0, keepdims=True)
            for part in parts[1:]:
                total = total + jnp.sum(part, axis=0, keepdims=True)
            inverse = 1.0 / total
            out = jnp.zeros((BLOCK, 128), f32)
            for kb in range(b + 1):
                prob = parts[kb] * inverse
                PT[tile(b, kb)] = prob
                out = out + tn(prob.astype(bf16), two(VU, kb))
            OS[2 * b : 2 * b + 2] = out.astype(bf16).reshape(2, 192, 128)
            for s in (2 * b, 2 * b + 1):
                from_host(OS, OB, oi, oh + s, s)

    b_arrived(-4)
    b_to_x(-4)
    for h in (0, 1):
        a_arrived(-2, h)
        a_up(-2, h)
        a_arrived(2, h)
        a_down(2, h)
    x_relay(-3)
    x_relay(3)
    x_relay(-4)

    arrived(GB.at[across, half[0]], gi + 3)
    go(GB.at[across, half[0]], GB.at[across, half[0]], gi + 7, ctx, partner)
    arrived(GB.at[across, half[1]], gi + 5)
    go(GB.at[across, half[1]], GB.at[across, half[1]], gi + 8, ctx, partner)
    back_base = sum_middle(0, back_base, adapter_scale)

    a_arrived(-3, 0)
    a_up(-3, 0)
    a_arrived(-3, 1)
    a_arrived(3, 1)
    a_down(3, 1)
    a_arrived(3, 0)

    for head in range(4):
        arrived(OB.at[:, head * 128 : (head + 1) * 128], oi + head)
    mid_base = sum_start(1, nt(OB[...], down_full))
    lora_back = sum_end(0, back_base)

    arrived(GB.at[partner], gi)
    arrived(GB.at[(partner + 6) % 8], gi + 4)
    arrived(GB.at[(partner + 2) % 8], gi + 6)
    arrived(GB.at[(partner + 4) % 8, half[0]], gi + 7)
    arrived(GB.at[(partner + 4) % 8, half[1]], gi + 8)

    def a_part(d):
        yy = row(d)
        return nn(GB[yy], WA[yy].reshape(640, 256))

    total_a = nn(lora_back, down_full[:, :256])
    total_b = nn(lora_back, down_full[:, 256:])
    for d in (0, -1, 1, -2, 2, -3, 3):
        total_a = total_a + a_part(d)

    mid_base = sum_middle(1, mid_base, 1.0)

    a_arrived(-4, 0)
    a_arrived(4, 1)
    total_a = total_a + a_part(4)
    DOB[:, 0:256] = total_a.astype(bf16)

    for d in range(-4, 4):
        far = 1 if d in up_relay else -1
        arrived(PB(d, far), xb[(far, d)])
        arrived(PB(d, 2), xr[d])
    for yy in range(8):
        total_b = total_b + nn(GB[yy], WB[yy].reshape(640, 256))
    DOB[:, 256:512] = total_b.astype(bf16)
    to_hosts(DOB, DU, di)

    lora_mid = sum_end(1, mid_base)
    UPD[:, :, 0:512] = tn(lora_back, OB[...])[:64].reshape(8, 8, 512)
    UPD[:, :, 512:1152] = (adapter_scale * tn(lora_mid, g_ref[...]))[:64].reshape(8, 8, 640)
    ri = ids(8)
    for j in range(1, 8):
        go(UPD.at[row(j)], R1.at[y], ri + j, ydev(j), f)

    gq, gk, gv = ids(4), ids(4), ids(4)
    hq, hk, hv = ids(8), ids(8), ids(8)

    @pl.when(is_host)
    def _():
        for kb in range(blocks):
            KT[:, kb * BLOCK : (kb + 1) * BLOCK] = two(KU, kb).astype(f32).T.astype(bf16)
        DKA[...] = jnp.zeros_like(DKA)
        DVA[...] = jnp.zeros_like(DVA)
        for s in range(8):
            arrived(DU.at[s], di + s)
        for b in reversed(range(blocks)):
            grad, query = two(DU, b), two(QU, b)
            parts = []
            delta = jnp.zeros((1, BLOCK), f32)
            for kb in range(b + 1):
                part = nt(two(VU, kb), grad)
                delta = delta + jnp.sum(PT[tile(b, kb)] * part, axis=0, keepdims=True)
                parts.append(part)
            turned = jnp.zeros((128, BLOCK), f32)
            for kb in range(b + 1):
                span = pl.ds(kb * BLOCK, BLOCK)
                prob = PT[tile(b, kb)]
                pull = (prob * (parts[kb] - delta) * scale).astype(bf16)
                DKA[span] += nn(pull, query)
                DVA[span] += nn(prob.astype(bf16), grad)
                turned = turned + nn(KT[:, span], pull)
            span = pl.ds(b * BLOCK, BLOCK)
            DQS[2 * b : 2 * b + 2] = turned.T.astype(bf16).reshape(2, 192, 128)
            DKS[2 * b : 2 * b + 2] = DKA[span].astype(bf16).reshape(2, 192, 128)
            DVS[2 * b : 2 * b + 2] = DVA[span].astype(bf16).reshape(2, 192, 128)
            for s in (2 * b, 2 * b + 1):
                from_host(DQS, dq_ref, gq, hq + s, s)
                from_host(DKS, dk_ref, gk, hk + s, s)
                from_host(DVS, dv_ref, gv, hv + s, s)

    total = UPD[y]
    for j in range(1, 8):
        frm = row(8 - j)
        arrived(R1.at[frm], ri + j)
        total = total + R1[frm]
    for j in range(8):
        S2[j] = total[j : j + 1]
    ti = ids(8)
    for j in range(1, 8):
        to = (g + j) % 8
        go(S2.at[to], R2.at[g], ti + j, at(y, to), f)
    total = S2[g]
    for j in range(1, 8):
        frm = (g + 8 - j) % 8
        arrived(R2.at[frm], ti + j)
        total = total + R2[frm]
    dn_ref[...] = total[:, 0:512]
    up_ref[...] = total[:, 512:1152]

    for head in range(4):
        span = slice(head * 128, (head + 1) * 128)
        arrived(dq_ref.at[:, span], gq + head)
        arrived(dk_ref.at[:, span], gk + head)
        arrived(dv_ref.at[:, span], gv + head)

    for copy in sends:
        copy.wait_send()
    for away, copy in conditional:

        @pl.when(away)
        def _(copy=copy):
            copy.wait_send()

    @pl.when(is_host)
    def _():
        for what in hosted:
            away, copy, _, _ = returned(*what)

            @pl.when(away)
            def _(copy=copy):
                copy.wait_send()

    assert counter[0] <= SEMS


def on_device(q, k, v, grad, codes, index, table, down, up):
    weight = dequantize(codes, index, table)
    vmem = pl.BlockSpec(memory_space=pltpu.VMEM)
    tokens, width = q.shape
    out = jax.ShapeDtypeStruct((tokens, width), bf16)
    slabs = pltpu.VMEM((8, 192, 128), bf16)
    results = pl.pallas_call(
        kernel,
        name="block_backward",
        out_shape=(
            out,
            out,
            out,
            jax.ShapeDtypeStruct((1, width), f32),
            jax.ShapeDtypeStruct((1, grad.shape[1]), f32),
        ),
        in_specs=[vmem] * 7,
        out_specs=[vmem] * 5,
        scratch_shapes=[
            pltpu.VMEM((8, 8, 80, 256), bf16),
            pltpu.VMEM((8, 8, 80, 256), bf16),
            pltpu.VMEM((8, 192, 640), bf16),
            slabs,
            slabs,
            slabs,
            slabs,
            pltpu.VMEM((10, BLOCK, BLOCK), f32),
            pltpu.VMEM((128, 1536), bf16),
            pltpu.VMEM((192, 512), bf16),
            slabs,
            slabs,
            slabs,
            slabs,
            pltpu.VMEM((1536, 128), f32),
            pltpu.VMEM((1536, 128), f32),
            pltpu.VMEM((192, 512), bf16),
            pltpu.VMEM((8, 1, 1152), f32),
            pltpu.VMEM((8, 8, 1152), f32),
            pltpu.VMEM((2, 8, 24, 128), f32),
            pltpu.VMEM((2, 8, 24, 128), f32),
            pltpu.VMEM((2, 8, 24, 128), f32),
            pltpu.VMEM((8, 8, 1152), f32),
            pltpu.VMEM((8, 8, 1152), f32),
            pltpu.VMEM((8, 1, 1152), f32),
            pltpu.VMEM((8, 1, 1152), f32),
            pltpu.SemaphoreType.DMA((SEMS,)),
            pltpu.SemaphoreType.DMA((SEMS,)),
            pltpu.SemaphoreType.DMA((3,)),
        ],
        compiler_params=pltpu.CompilerParams(
            collective_id=0, has_side_effects=True, vmem_limit_bytes=56 * 1024 * 1024
        ),
    )(q, k, v, grad, weight, down, up)
    return results


def solution(mesh):
    spec = P("ctx", "fsdp")
    return jax.shard_map(
        on_device,
        mesh=mesh,
        in_specs=(spec, spec, spec, spec, spec, spec, P(), spec, spec),
        out_specs=(spec,) * 5,
        check_vma=False,
    )
```

```python
import jax
import jax.numpy as jnp
from jax import lax
from jax.experimental import pallas as pl
from jax.experimental.pallas import tpu as pltpu
from jax.sharding import PartitionSpec as P

HEAD_WIDTH = 128
MESH = pl.DeviceIdType.MESH
BLOCK = 384
nf4_values = (
    -1.0,
    -0.6961928009986877,
    -0.5250730514526367,
    -0.39491748809814453,
    -0.28444138169288635,
    -0.18477343022823334,
    -0.09105003625154495,
    0.0,
    0.07958029955625534,
    0.16093020141124725,
    0.24611230194568634,
    0.33791524171829224,
    0.44070982933044434,
    0.5626170039176941,
    0.7229568362236023,
    1.0,
)
adapter_scale = 0.25
masked = -1e30
f32, bf16 = jnp.float32, jnp.bfloat16
SENDS, RECVS = 24, 64


def nt(a, b):
    return lax.dot_general(a, b, (((1,), (1,)), ((), ())), preferred_element_type=f32)


def tn(a, b):
    return lax.dot_general(a, b, (((0,), (0,)), ((), ())), preferred_element_type=f32)


def nn(a, b):
    return jnp.dot(a, b, preferred_element_type=f32)


def kernel(
    codes_ref, index_ref, table_ref, ad_ref, au_ref, q_ref, k_ref, v_ref, g_ref,
    dq_ref, dk_ref, dv_ref, dn_ref, up_ref,
    WA, WB, GB, QU, KU, VU, DU, PT, KT, OB, OS, DQS, DKS, DVS, DKA, DVA, DOB,
    AD1, AD2, PSS, PSR, PSG, UPD, R1, S2, R2, ss, rs, ls,
):
    ctx = lax.axis_index("ctx")
    f = lax.axis_index("fsdp")
    y, g = ctx // 8, ctx % 8
    x, zl = g // 2, g % 2
    c = f % 2
    partner = f + 1 - 2 * c
    scale = HEAD_WIDTH ** (-0.5)
    is_host = (x % 2) == c
    unit_head = 2 * (x // 2) + zl


    sent, heard = [0], [0]

    def send_id():
        sent[0] += 1
        return sent[0] - 1

    def recv_id():
        heard[0] += 1
        return heard[0] - 1

    def remote(src, dst, send, recv, to_ctx, to_f):
        return pltpu.make_async_remote_copy(
            src_ref=src,
            dst_ref=dst,
            send_sem=ss.at[send],
            recv_sem=rs.at[recv],
            device_id={"ctx": to_ctx, "fsdp": to_f},
            device_id_type=MESH,
        )

    def go(src, send, recv, to_ctx, to_f, dst=None):
        remote(src, src if dst is None else dst, send, recv, to_ctx, to_f).start()

    def arrived(dst, recv):
        pltpu.make_async_copy(dst, dst, rs.at[recv]).wait()

    def left(src, send):
        pltpu.make_async_copy(src, src, ss.at[send]).wait()

    def row(dy):
        return (y + dy) % 8

    def at(yy, gg):
        return yy * 8 + gg

    def ydev(dy):
        return at(row(dy), g)

    def xdev(dx):
        return at(y, ((x + dx) % 4) * 2 + zl)

    def fdev(df):
        return (f + df) % 8

    other_row = jnp.where(x < 2, (y + 7) % 8, (y + 1) % 8)
    other_g = jnp.where(x < 2, 4, 0)

    barrier = pltpu.get_barrier_semaphore()
    peers = [(at(y, (g + j) % 8), f) for j in range(1, 8)]
    peers += [(ydev(j), f) for j in range(1, 8)]
    peers += [(ctx, fdev(j)) for j in range(1, 8)]
    peers += [(at(other_row, other_g + j), f) for j in range(4)]
    for to_ctx, to_f in peers:
        pl.semaphore_signal(
            barrier, inc=1, device_id={"ctx": to_ctx, "fsdp": to_f}, device_id_type=MESH
        )
    own_grad = pltpu.make_async_copy(g_ref, GB.at[f], ls.at[0])
    own_grad.start()

    codes = codes_ref[...]
    values = jnp.zeros(codes.shape, f32)
    for level in range(16):
        values = jnp.where(codes == level, nf4_values[level], values)
    table = table_ref[...]
    level_at = lax.broadcasted_iota(jnp.int32, (codes.shape[0], table.shape[1]), 1)
    block_at = lax.broadcasted_iota(jnp.int32, codes.shape, 1) // 64
    scales = jnp.zeros(codes.shape, f32)
    for block in range(8):
        picked = jnp.where(index_ref[:, block : block + 1] == level_at, table, 0.0)
        picked = jnp.sum(picked, axis=1, keepdims=True)
        scales = jnp.where(block_at == block, picked, scales)
    weight = (values * scales).astype(bf16)
    WA[y, g] = weight[:, :256]
    WB[y, g] = weight[:, 256:]
    AD1[g] = jnp.concatenate([ad_ref[...].astype(f32), au_ref[...].astype(f32)], axis=1)
    pl.semaphore_wait(barrier, len(peers))

    pair = ctx + 1 - 2 * zl
    first, few = recv_id(), send_id()
    go(WA.at[y, g], few, first, pair, f)
    go(WB.at[y, g], few, first, pair, f)

    ad1_s, ad1_r = send_id(), recv_id()
    for j in range(1, 8):
        go(AD1.at[g], ad1_s, ad1_r, at(y, (g + j) % 8), f)

    def PB(dy, dx):
        return WB.at[row(dy), pl.ds(((x + dx) % 4) * 2, 2)]

    def QA(dy, h):
        return WA.at[row(dy), pl.ds(4 * h, 4)]

    up_relay = (-2, -1, 0, 1)
    yb = {d: recv_id() for d in (-4, -3, -2, -1, 1, 2, 3)}
    xlast = recv_id()
    xb = {}
    for d in range(-4, 4):
        xb[(-1, d)] = recv_id() if d in up_relay else xlast
        xb[(1, d)] = xlast if d in up_relay else recv_id()
    all_b, all_a = send_id(), send_id()

    def b_to_x(d):
        go(PB(d, 0), all_b, xb[(-1, d)], xdev(1), f)
        go(PB(d, 0), all_b, xb[(1, d)], xdev(-1), f)

    def b_up(d):
        go(PB(d, 0), all_b, yb[d - 1], ydev(1), f)

    def b_down(d):
        go(PB(d, 0), all_b, yb[d + 1], ydev(-1), f)

    def x_relay(d):
        side = -1 if d in up_relay else 1
        arrived(PB(d, side), xb[(side, d)])
        go(PB(d, side), all_b, xlast, xdev(-side), f)

    ya = {(d, h): recv_id() for d in (-3, -2, -1, 1, 2, 3) for h in (0, 1)}
    ya[(-4, 0)] = recv_id()
    ya[(4, 1)] = recv_id()

    def a_up(d, h):
        go(QA(d, h), all_a, ya[(d - 1, h)], ydev(1), f)

    def a_down(d, h):
        go(QA(d, h), all_a, ya[(d + 1, h)], ydev(-1), f)

    def a_arrived(d, h):
        arrived(QA(d, h), ya[(d, h)])

    def a_step(d, h):
        a_arrived(-d, h)
        if d < 3 or h == 0:
            a_up(-d, h)
        a_arrived(d, h)
        if d < 3 or h == 1:
            a_down(d, h)

    def b_step(d):
        arrived(PB(-d, 0), yb[-d])
        b_up(-d)
        b_to_x(-d)
        arrived(PB(d, 0), yb[d])
        if d < 3:
            b_down(d)
        b_to_x(d)

    arrived(WA.at[0, pl.ds(0, 2)], first)
    b_up(0)
    b_down(0)
    mine = WA.at[y, pl.ds(x * 2, 2)]
    xa = recv_id()
    go(mine, few, xa, xdev(1), f)
    go(mine, few, xa, xdev(-1), f)
    go(mine, all_b, xa, xdev(2), f)
    b_to_x(0)

    half = [pl.ds(0, 96), pl.ds(96, 96)]
    gs = send_id()
    g_own, g_low, g_high, g_low_half, g_high_half, g_rest = [recv_id() for _ in range(6)]
    own_grad.wait()
    go(GB.at[f], gs, g_low, ctx, fdev(2))
    go(GB.at[f], gs, g_high, ctx, fdev(6))
    go(GB.at[f], gs, g_rest, ctx, partner)

    def slab_of(head):
        if head < 2:
            return y, g
        return jnp.where(x < 2, (y + 7) % 8, y), (g + 4) % 8

    def host_of(head):
        yy, _ = slab_of(head)
        return at(yy, (2 * (head // 2) + c) * 2 + head % 2)

    to_host_sends = []

    def to_hosts(src_ref, dst_buf, recv):
        send = send_id()
        to_host_sends.append(send)
        for head in range(4):
            dest = host_of(head)
            _, slot = slab_of(head)
            src = src_ref.at[:, head * 128 : (head + 1) * 128]
            dst = dst_buf.at[slot]
            away = dest != ctx

            @pl.when(away)
            def _():
                go(src, send, recv, dest, f, dst)

            @pl.when(jnp.logical_not(away))
            def _():
                pltpu.make_async_copy(src, dst, rs.at[recv]).start()

    ki, qi, vi, di = [recv_id() for _ in range(4)]
    to_hosts(k_ref, KU, ki)
    to_hosts(q_ref, QU, qi)
    to_hosts(v_ref, VU, vi)

    arrived(AD1.at[pl.ds(0, 7)], ad1_r)
    AD2[y] = jnp.concatenate([AD1[j] for j in range(8)], axis=0)
    ad2_s, ad2_r = send_id(), recv_id()
    for j in range(1, 8):
        go(AD2.at[y], ad2_s, ad2_r, ydev(j), f)

    arrived(WA.at[0, pl.ds(0, 6)], xa)
    a_up(0, 0)
    a_down(0, 0)

    b_step(1)
    x_relay(0)
    a_up(0, 1)
    a_down(0, 1)

    b_step(2)
    x_relay(-1)
    x_relay(1)
    a_step(1, 0)

    below, above, across = fdev(6), fdev(2), fdev(4)
    arrived(GB.at[below], g_low)
    go(GB.at[below, half[0]], gs, g_low_half, ctx, above)
    go(GB.at[below], gs, g_rest, ctx, partner)
    arrived(GB.at[above], g_high)
    go(GB.at[above, half[1]], gs, g_high_half, ctx, below)
    go(GB.at[above], gs, g_rest, ctx, partner)

    def sum_start(n, piece):
        PSS[n] = piece.reshape(8, 24, 128)
        send, recv = send_id(), recv_id()
        for j in range(1, 8):
            to = fdev(j)
            go(PSS.at[n, to], send, recv, ctx, to, PSR.at[n, f])
        return send, recv

    def sum_middle(n, pair, factor):
        arrived(PSR.at[n, pl.ds(0, 7)], pair[1])
        total = PSS[n, f]
        for j in range(1, 8):
            total = total + PSR[n, fdev(j)]
        PSG[n, f] = (total * factor).astype(bf16).astype(f32)
        send, recv = send_id(), recv_id()
        for j in range(1, 8):
            go(PSG.at[n, f], send, recv, ctx, fdev(j))
        return send, recv

    def sum_end(n, pair):
        arrived(PSG.at[n, pl.ds(0, 7)], pair[1])
        return PSG[n].reshape(192, 128).astype(bf16)

    arrived(AD2.at[pl.ds(0, 7)], ad2_r)
    adapters = AD2[...].reshape(64, 1152).astype(bf16)
    adapters = jnp.concatenate([adapters, jnp.zeros_like(adapters)], axis=0)
    down_full, up_piece = adapters[:, :512], adapters[:, 512:]
    back0 = sum_start(0, nt(GB[f], up_piece))

    def source_of(slot):
        if slot < 4:
            return jnp.where(x < 2, at(y, slot), at(y, slot + 4))
        return jnp.where(x < 2, at(y, slot), at(row(1), slot - 4))

    head_columns = pl.ds(pl.multiple_of(unit_head * 128, 128), 128)

    def from_host(buf, dst_ref, send, recv, slot):
        dest = source_of(slot)
        src, dst = buf.at[slot], dst_ref.at[:, head_columns]
        away = dest != ctx

        @pl.when(away)
        def _():
            go(src, send, recv, dest, f, dst)

        @pl.when(jnp.logical_not(away))
        def _():
            pltpu.make_async_copy(src, dst, rs.at[recv]).start()

    blocks = 1536 // BLOCK

    def two(buf, b):
        return buf[2 * b : 2 * b + 2].reshape(BLOCK, 128)

    def tile(b, kb):
        return b * (b + 1) // 2 + kb

    oh, oi = send_id(), recv_id()

    def forward(b):
        key_at = lax.broadcasted_iota(jnp.int32, (BLOCK, BLOCK), 0)
        query_at = lax.broadcasted_iota(jnp.int32, (BLOCK, BLOCK), 1)
        seen = key_at <= query_at
        query = two(QU, b)
        parts = []
        for kb in range(b + 1):
            part = nt(two(KU, kb), query) * scale
            parts.append(jnp.where(seen, part, masked) if kb == b else part)
        top = jnp.max(parts[0], axis=0, keepdims=True)
        for part in parts[1:]:
            top = jnp.maximum(top, jnp.max(part, axis=0, keepdims=True))
        parts = [jnp.exp(part - top) for part in parts]
        total = jnp.sum(parts[0], axis=0, keepdims=True)
        for part in parts[1:]:
            total = total + jnp.sum(part, axis=0, keepdims=True)
        inverse = 1.0 / total
        out = jnp.zeros((BLOCK, 128), f32)
        for kb in range(b + 1):
            prob = parts[kb] * inverse
            PT[tile(b, kb)] = prob
            out = out + tn(prob.astype(bf16), two(VU, kb))
        OS[2 * b : 2 * b + 2] = out.astype(bf16).reshape(2, 192, 128)
        for s in (2 * b, 2 * b + 1):
            from_host(OS, OB, oh, oi, s)

    b_step(3)
    x_relay(-2)
    x_relay(2)
    a_step(1, 1)


    @pl.when(is_host)
    def _():
        arrived(KU, ki)
        arrived(QU, qi)
        arrived(VU, vi)
        for b in (0, 1):
            forward(b)

    arrived(PB(-4, 0), yb[-4])
    b_to_x(-4)
    x_relay(-3)
    x_relay(3)
    a_step(2, 0)


    @pl.when(is_host)
    def _():
        forward(2)

    back0 = (back0, sum_middle(0, back0, adapter_scale))
    x_relay(-4)
    a_step(2, 1)

    @pl.when(is_host)
    def _():
        forward(3)

    arrived(GB.at[across, half[0]], g_low_half)
    go(GB.at[across, half[0]], gs, g_rest, ctx, partner)
    arrived(GB.at[across, half[1]], g_high_half)
    go(GB.at[across, half[1]], gs, g_rest, ctx, partner)

    a_step(3, 0)
    a_step(3, 1)

    arrived(OB, oi)
    mid0 = sum_start(1, nt(OB[...], down_full))
    lora_back = sum_end(0, back0[1])
    UPD[:, :, 0:512] = tn(lora_back, OB[...])[:64].reshape(8, 8, 512)
    total_a = nn(lora_back, down_full[:, :256])
    total_b = nn(lora_back, down_full[:, 256:])

    arrived(GB.at[pl.ds(0, 4)], g_rest)

    def a_part(d):
        yy = row(d)
        return nn(GB[yy], WA[yy].reshape(640, 256))

    mid1 = sum_middle(1, mid0, 1.0)
    for d in (0, -1, 1, -2, 2, -3, 3):
        total_a = total_a + a_part(d)

    lora_mid = sum_end(1, mid1)
    UPD[:, :, 512:1152] = (adapter_scale * tn(lora_mid, GB[f]))[:64].reshape(8, 8, 640)
    rs1_s, rs1_r = send_id(), recv_id()
    for j in range(1, 8):
        go(UPD.at[row(j)], rs1_s, rs1_r, ydev(j), f, R1.at[y])

    a_arrived(-4, 0)
    a_arrived(4, 1)
    total_a = total_a + a_part(4)
    DOB[:, 0:256] = total_a.astype(bf16)

    arrived(WB.at[pl.ds(0, 4)], xlast)
    for yy in range(8):
        total_b = total_b + nn(GB[yy], WB[yy].reshape(640, 256))
    DOB[:, 256:512] = total_b.astype(bf16)
    to_hosts(DOB, DU, di)

    arrived(R1.at[pl.ds(0, 7)], rs1_r)
    total = UPD[y]
    for j in range(1, 8):
        total = total + R1[row(j)]
    for j in range(8):
        S2[j] = total[j : j + 1]
    rs2_s, rs2_r = send_id(), recv_id()
    for j in range(1, 8):
        to = (g + j) % 8
        go(S2.at[to], rs2_s, rs2_r, at(y, to), f, R2.at[g])

    gq, gk, gv = [recv_id() for _ in range(3)]
    hq, hk, hv = [send_id() for _ in range(3)]


    @pl.when(is_host)
    def _():
        for kb in range(blocks):
            KT[:, kb * BLOCK : (kb + 1) * BLOCK] = two(KU, kb).astype(f32).T.astype(bf16)
        DKA[...] = jnp.zeros_like(DKA)
        DVA[...] = jnp.zeros_like(DVA)
        arrived(DU, di)
        for b in reversed(range(blocks)):
            grad, query = two(DU, b), two(QU, b)
            parts = []
            delta = jnp.zeros((1, BLOCK), f32)
            for kb in range(b + 1):
                part = nt(two(VU, kb), grad)
                delta = delta + jnp.sum(PT[tile(b, kb)] * part, axis=0, keepdims=True)
                parts.append(part)
            turned = jnp.zeros((128, BLOCK), f32)
            for kb in range(b + 1):
                span = pl.ds(kb * BLOCK, BLOCK)
                prob = PT[tile(b, kb)]
                pull = (prob * (parts[kb] - delta) * scale).astype(bf16)
                DKA[span] += nn(pull, query)
                DVA[span] += nn(prob.astype(bf16), grad)
                turned = turned + nn(KT[:, span], pull)
            span = pl.ds(b * BLOCK, BLOCK)
            DQS[2 * b : 2 * b + 2] = turned.T.astype(bf16).reshape(2, 192, 128)
            DKS[2 * b : 2 * b + 2] = DKA[span].astype(bf16).reshape(2, 192, 128)
            DVS[2 * b : 2 * b + 2] = DVA[span].astype(bf16).reshape(2, 192, 128)
            for s in (2 * b, 2 * b + 1):
                from_host(DQS, dq_ref, hq, gq, s)
                from_host(DKS, dk_ref, hk, gk, s)
                from_host(DVS, dv_ref, hv, gv, s)

    arrived(R2.at[pl.ds(0, 7)], rs2_r)
    total = S2[g]
    for j in range(1, 8):
        total = total + R2[(g + j) % 8]
    dn_ref[...] = total[:, 0:512]
    up_ref[...] = total[:, 512:1152]

    arrived(dq_ref, gq)
    arrived(dk_ref, gk)
    arrived(dv_ref, gv)

    seven = pl.ds(0, 7)
    left(WA.at[0, pl.ds(0, 6)], few)
    left(WB, all_b)
    left(WA.at[seven], all_a)
    left(GB.at[seven], gs)
    left(AD1.at[seven], ad1_s)
    left(AD2.at[seven], ad2_s)
    left(PSS.at[0, seven], back0[0][0])
    left(PSG.at[0, seven], back0[1][0])
    left(PSS.at[1, seven], mid0[0])
    left(PSG.at[1, seven], mid1[0])
    left(UPD.at[seven], rs1_s)
    left(S2.at[seven], rs2_s)

    @pl.when(is_host)
    def _():
        for send in to_host_sends:
            left(KU.at[pl.ds(0, 3)], send)
        for send in (oh, hq, hk, hv):
            left(OS.at[seven], send)

    @pl.when(jnp.logical_not(is_host))
    def _():
        for send in to_host_sends:
            left(KU.at[pl.ds(0, 4)], send)

    assert sent[0] <= SENDS and heard[0] <= RECVS, (sent, heard)


def finish_kernel(*refs):
    for src, dst in zip(refs[:5], refs[5:]):
        dst[...] = src[...]


def on_device(q, k, v, grad, codes, index, table, down, up):
    vmem = pl.BlockSpec(memory_space=pltpu.VMEM)
    tokens, width = q.shape
    out = jax.ShapeDtypeStruct((tokens, width), bf16)
    slabs = pltpu.VMEM((8, 192, 128), bf16)
    results = pl.pallas_call(
        kernel,
        name="block_backward",
        out_shape=(
            out,
            out,
            out,
            jax.ShapeDtypeStruct((1, width), f32),
            jax.ShapeDtypeStruct((1, grad.shape[1]), f32),
        ),
        in_specs=[vmem] * 5 + [pl.BlockSpec(memory_space=pl.ANY)] * 4,
        out_specs=[vmem] * 5,
        scratch_shapes=[
            pltpu.VMEM((8, 8, 80, 256), bf16),
            pltpu.VMEM((8, 8, 80, 256), bf16),
            pltpu.VMEM((8, 192, 640), bf16),
            slabs,
            slabs,
            slabs,
            slabs,
            pltpu.VMEM((10, BLOCK, BLOCK), f32),
            pltpu.VMEM((128, 1536), bf16),
            pltpu.VMEM((192, 512), bf16),
            slabs,
            slabs,
            slabs,
            slabs,
            pltpu.VMEM((1536, 128), f32),
            pltpu.VMEM((1536, 128), f32),
            pltpu.VMEM((192, 512), bf16),
            pltpu.VMEM((8, 1, 1152), f32),
            pltpu.VMEM((8, 8, 1152), f32),
            pltpu.VMEM((2, 8, 24, 128), f32),
            pltpu.VMEM((2, 8, 24, 128), f32),
            pltpu.VMEM((2, 8, 24, 128), f32),
            pltpu.VMEM((8, 8, 1152), f32),
            pltpu.VMEM((8, 8, 1152), f32),
            pltpu.VMEM((8, 1, 1152), f32),
            pltpu.VMEM((8, 1, 1152), f32),
            pltpu.SemaphoreType.DMA((SENDS,)),
            pltpu.SemaphoreType.DMA((RECVS,)),
            pltpu.SemaphoreType.DMA((1,)),
        ],
        compiler_params=pltpu.CompilerParams(
            collective_id=0, has_side_effects=True, vmem_limit_bytes=56 * 1024 * 1024
        ),
    )(codes, index, table.reshape(1, -1), down, up, q, k, v, grad)
    return pl.pallas_call(
        finish_kernel,
        name="finish",
        out_shape=tuple(jax.ShapeDtypeStruct(r.shape, r.dtype) for r in results),
        in_specs=[vmem] * 5,
        out_specs=[vmem] * 5,
    )(*results)


def solution(mesh):
    spec = P("ctx", "fsdp")
    return jax.shard_map(
        on_device,
        mesh=mesh,
        in_specs=(spec, spec, spec, spec, spec, spec, P(), spec, spec),
        out_specs=(spec,) * 5,
        check_vma=False,
    )
```

```python
import jax
import jax.numpy as jnp
from jax import lax
from jax.experimental import pallas as pl
from jax.experimental.pallas import tpu as pltpu
from jax.sharding import PartitionSpec as P

HEAD_WIDTH = 128
MESH = pl.DeviceIdType.MESH
BLOCK = 384
nf4_values = (
    -1.0,
    -0.6961928009986877,
    -0.5250730514526367,
    -0.39491748809814453,
    -0.28444138169288635,
    -0.18477343022823334,
    -0.09105003625154495,
    0.0,
    0.07958029955625534,
    0.16093020141124725,
    0.24611230194568634,
    0.33791524171829224,
    0.44070982933044434,
    0.5626170039176941,
    0.7229568362236023,
    1.0,
)
adapter_scale = 0.25
masked = -1e30
f32, bf16 = jnp.float32, jnp.bfloat16
SENDS, RECVS = 24, 64


def nt(a, b):
    return lax.dot_general(a, b, (((1,), (1,)), ((), ())), preferred_element_type=f32)


def tn(a, b):
    return lax.dot_general(a, b, (((0,), (0,)), ((), ())), preferred_element_type=f32)


def nn(a, b):
    return jnp.dot(a, b, preferred_element_type=f32)


def kernel(
    codes_ref, index_ref, table_ref, ad_ref, au_ref, q_ref, k_ref, v_ref, g_ref,
    dq_ref, dk_ref, dv_ref, dn_ref, up_ref,
    WA, WB, GB, QU, KU, VU, DU, PT, KT, OB, OS, DQS, DKS, DVS, DKA, DVA, DOB,
    AD1, AD2, PSS, PSR, PSG, UPD, R1, S2, R2, ss, rs, ls,
):
    ctx = lax.axis_index("ctx")
    f = lax.axis_index("fsdp")
    y, g = ctx // 8, ctx % 8
    x, zl = g // 2, g % 2
    c = f % 2
    partner = f + 1 - 2 * c
    scale = HEAD_WIDTH ** (-0.5)
    shifted_x = 3 * (1 - c)
    shifted_host = x == shifted_x
    is_host = jnp.logical_or(x == 1 + c, shifted_host)
    unit_head = jnp.where(shifted_host, 2, 0) + zl


    sent, heard = [0], [0]

    def send_id():
        sent[0] += 1
        return sent[0] - 1

    def recv_id():
        heard[0] += 1
        return heard[0] - 1

    def remote(src, dst, send, recv, to_ctx, to_f):
        return pltpu.make_async_remote_copy(
            src_ref=src,
            dst_ref=dst,
            send_sem=ss.at[send],
            recv_sem=rs.at[recv],
            device_id={"ctx": to_ctx, "fsdp": to_f},
            device_id_type=MESH,
        )

    def go(src, send, recv, to_ctx, to_f, dst=None):
        remote(src, src if dst is None else dst, send, recv, to_ctx, to_f).start()

    def arrived(dst, recv):
        pltpu.make_async_copy(dst, dst, rs.at[recv]).wait()

    def left(src, send):
        pltpu.make_async_copy(src, src, ss.at[send]).wait()

    def row(dy):
        return (y + dy) % 8

    def at(yy, gg):
        return yy * 8 + gg

    def ydev(dy):
        return at(row(dy), g)

    def xdev(dx):
        return at(y, ((x + dx) % 4) * 2 + zl)

    def fdev(df):
        return (f + df) % 8

    other_row = jnp.where(x < 2, (y + 7) % 8, (y + 1) % 8)
    other_g = jnp.where(x < 2, 4, 0)

    barrier = pltpu.get_barrier_semaphore()
    peers = [(at(y, (g + j) % 8), f) for j in range(1, 8)]
    peers += [(ydev(j), f) for j in range(1, 8)]
    peers += [(ctx, fdev(j)) for j in range(1, 8)]
    peers += [(at(other_row, other_g + j), f) for j in range(4)]
    for to_ctx, to_f in peers:
        pl.semaphore_signal(
            barrier, inc=1, device_id={"ctx": to_ctx, "fsdp": to_f}, device_id_type=MESH
        )
    own_grad = pltpu.make_async_copy(g_ref, GB.at[f], ls.at[0])
    own_grad.start()

    codes = codes_ref[...]
    values = jnp.zeros(codes.shape, f32)
    for level in range(16):
        values = jnp.where(codes == level, nf4_values[level], values)
    table = table_ref[...]
    index = jnp.concatenate([index_ref[...].astype(f32), jnp.zeros((8, 48), f32)], axis=1)
    index = index.T[: codes.shape[0]].astype(jnp.int32)
    level_at = lax.broadcasted_iota(jnp.int32, (codes.shape[0], table.shape[1]), 1)
    block_at = lax.broadcasted_iota(jnp.int32, codes.shape, 1) // 64
    scales = jnp.zeros(codes.shape, f32)
    for block in range(8):
        picked = jnp.where(index[:, block : block + 1] == level_at, table, 0.0)
        picked = jnp.sum(picked, axis=1, keepdims=True)
        scales = jnp.where(block_at == block, picked, scales)
    weight = (values * scales).astype(bf16)
    WA[y, g] = weight[:, :256]
    WB[y, g] = weight[:, 256:]
    AD1[g] = jnp.concatenate([ad_ref[...].astype(f32), au_ref[...].astype(f32)], axis=1)
    pl.semaphore_wait(barrier, len(peers))

    pair = ctx + 1 - 2 * zl
    first, few = recv_id(), send_id()
    go(WA.at[y, g], few, first, pair, f)
    go(WB.at[y, g], few, first, pair, f)

    ad1_s, ad1_r = send_id(), recv_id()
    for j in range(1, 8):
        go(AD1.at[g], ad1_s, ad1_r, at(y, (g + j) % 8), f)

    def PB(dy, dx):
        return WB.at[row(dy), pl.ds(((x + dx) % 4) * 2, 2)]

    def QA(dy, h):
        return WA.at[row(dy), pl.ds(4 * h, 4)]

    up_relay = (-2, -1, 0, 1)
    yb = {d: recv_id() for d in (-4, -3, -2, -1, 1, 2, 3)}
    xlast = recv_id()
    xb = {}
    for d in range(-4, 4):
        xb[(-1, d)] = recv_id() if d in up_relay else xlast
        xb[(1, d)] = xlast if d in up_relay else recv_id()
    all_b, all_a = send_id(), send_id()

    def b_to_x(d):
        go(PB(d, 0), all_b, xb[(-1, d)], xdev(1), f)
        go(PB(d, 0), all_b, xb[(1, d)], xdev(-1), f)

    def b_up(d):
        go(PB(d, 0), all_b, yb[d - 1], ydev(1), f)

    def b_down(d):
        go(PB(d, 0), all_b, yb[d + 1], ydev(-1), f)

    def x_relay(d):
        side = -1 if d in up_relay else 1
        arrived(PB(d, side), xb[(side, d)])
        go(PB(d, side), all_b, xlast, xdev(-side), f)

    ya = {(d, h): recv_id() for d in (-3, -2, -1, 1, 2, 3) for h in (0, 1)}
    ya[(-4, 0)] = recv_id()
    ya[(4, 1)] = recv_id()

    def a_up(d, h):
        go(QA(d, h), all_a, ya[(d - 1, h)], ydev(1), f)

    def a_down(d, h):
        go(QA(d, h), all_a, ya[(d + 1, h)], ydev(-1), f)

    def a_arrived(d, h):
        arrived(QA(d, h), ya[(d, h)])

    def a_step(d, h):
        a_arrived(-d, h)
        if d < 3 or h == 0:
            a_up(-d, h)
        a_arrived(d, h)
        if d < 3 or h == 1:
            a_down(d, h)

    def b_step(d):
        arrived(PB(-d, 0), yb[-d])
        b_up(-d)
        b_to_x(-d)
        arrived(PB(d, 0), yb[d])
        if d < 3:
            b_down(d)
        b_to_x(d)

    arrived(WA.at[0, pl.ds(0, 2)], first)
    b_up(0)
    b_down(0)
    mine = WA.at[y, pl.ds(x * 2, 2)]
    xa = recv_id()
    go(mine, few, xa, xdev(1), f)
    go(mine, few, xa, xdev(-1), f)
    go(mine, all_b, xa, xdev(2), f)
    b_to_x(0)

    half = [pl.ds(0, 96), pl.ds(96, 96)]
    gs = send_id()
    g_own, g_low, g_high, g_low_half, g_high_half, g_rest = [recv_id() for _ in range(6)]
    own_grad.wait()
    go(GB.at[f], gs, g_low, ctx, fdev(2))
    go(GB.at[f], gs, g_high, ctx, fdev(6))
    go(GB.at[f], gs, g_rest, ctx, partner)

    def slab_of(head):
        return g if head < 2 else (g + 4) % 8

    def host_of(head):
        if head < 2:
            return at(y, (1 + c) * 2 + head)
        first_row = jnp.where(x < 2, (y + 7) % 8, y)
        return at((first_row + c) % 8, shifted_x * 2 + head - 2)

    to_host_sends = []

    def to_hosts(src_ref, dst_buf, recv, send, heads):
        for head in heads:
            dest = host_of(head)
            slot = slab_of(head)
            src = src_ref.at[:, head * 128 : (head + 1) * 128]
            dst = dst_buf.at[slot]
            away = dest != ctx

            @pl.when(away)
            def _():
                go(src, send, recv, dest, f, dst)

            @pl.when(jnp.logical_not(away))
            def _():
                pltpu.make_async_copy(src, dst, rs.at[recv]).start()

    ki, qi, vi, di = [recv_id() for _ in range(4)]
    ks, qs, vs, ds = to_host_sends = [send_id() for _ in range(4)]

    def slabs():
        to_hosts(k_ref, KU, ki, ks, range(4))
        to_hosts(q_ref, QU, qi, qs, range(4))
        to_hosts(v_ref, VU, vi, vs, range(4))

    b_step(1)
    arrived(WA.at[0, pl.ds(0, 6)], xa)
    a_up(0, 0)
    a_down(0, 0)

    slabs()
    arrived(AD1.at[pl.ds(0, 7)], ad1_r)
    AD2[y] = jnp.concatenate([AD1[j] for j in range(8)], axis=0)
    ad2_s, ad2_r = send_id(), recv_id()
    for j in range(1, 8):
        go(AD2.at[y], ad2_s, ad2_r, ydev(j), f)

    x_relay(0)
    a_up(0, 1)
    a_down(0, 1)

    b_step(2)
    x_relay(-1)
    x_relay(1)
    a_step(1, 0)

    below, above, across = fdev(6), fdev(2), fdev(4)
    arrived(GB.at[below], g_low)
    go(GB.at[below, half[0]], gs, g_low_half, ctx, above)
    go(GB.at[below], gs, g_rest, ctx, partner)
    arrived(GB.at[above], g_high)
    go(GB.at[above, half[1]], gs, g_high_half, ctx, below)
    go(GB.at[above], gs, g_rest, ctx, partner)

    def sum_start(n, piece):
        PSS[n] = piece.reshape(8, 24, 128)
        send, recv = send_id(), recv_id()
        for j in range(1, 8):
            to = fdev(j)
            go(PSS.at[n, to], send, recv, ctx, to, PSR.at[n, f])
        return send, recv

    def sum_middle(n, pair, factor):
        arrived(PSR.at[n, pl.ds(0, 7)], pair[1])
        total = PSS[n, f]
        for j in range(1, 8):
            total = total + PSR[n, fdev(j)]
        PSG[n, f] = (total * factor).astype(bf16).astype(f32)
        send, recv = send_id(), recv_id()
        for j in range(1, 8):
            go(PSG.at[n, f], send, recv, ctx, fdev(j))
        return send, recv

    def sum_end(n, pair):
        arrived(PSG.at[n, pl.ds(0, 7)], pair[1])
        return PSG[n].reshape(192, 128).astype(bf16)

    arrived(AD2.at[pl.ds(0, 7)], ad2_r)
    adapters = AD2[...].reshape(64, 1152).astype(bf16)
    adapters = jnp.concatenate([adapters, jnp.zeros_like(adapters)], axis=0)
    down_full, up_piece = adapters[:, :512], adapters[:, 512:]
    back0 = sum_start(0, nt(GB[f], up_piece))

    first_row = (y + 8 - c) % 8

    def source_of(slot):
        if slot < 4:
            return jnp.where(shifted_host, at(first_row, slot + 4), at(y, slot))
        return jnp.where(shifted_host, at((first_row + 1) % 8, slot - 4), at(y, slot))

    head_columns = pl.ds(pl.multiple_of(unit_head * 128, 128), 128)

    def from_host(buf, dst_ref, send, recv, slot):
        dest = source_of(slot)
        src, dst = buf.at[slot], dst_ref.at[:, head_columns]
        away = dest != ctx

        @pl.when(away)
        def _():
            go(src, send, recv, dest, f, dst)

        @pl.when(jnp.logical_not(away))
        def _():
            pltpu.make_async_copy(src, dst, rs.at[recv]).start()

    blocks = 1536 // BLOCK

    def two(buf, b):
        return buf[2 * b : 2 * b + 2].reshape(BLOCK, 128)

    def tile(b, kb):
        return b * (b + 1) // 2 + kb

    oh, oi = send_id(), recv_id()

    def forward(b):
        key_at = lax.broadcasted_iota(jnp.int32, (BLOCK, BLOCK), 0)
        query_at = lax.broadcasted_iota(jnp.int32, (BLOCK, BLOCK), 1)
        seen = key_at <= query_at
        query = two(QU, b)
        parts = []
        for kb in range(b + 1):
            part = nt(two(KU, kb), query) * scale
            parts.append(jnp.where(seen, part, masked) if kb == b else part)
        top = jnp.max(parts[0], axis=0, keepdims=True)
        for part in parts[1:]:
            top = jnp.maximum(top, jnp.max(part, axis=0, keepdims=True))
        parts = [jnp.exp(part - top) for part in parts]
        total = jnp.sum(parts[0], axis=0, keepdims=True)
        for part in parts[1:]:
            total = total + jnp.sum(part, axis=0, keepdims=True)
        inverse = 1.0 / total
        out = jnp.zeros((BLOCK, 128), f32)
        for kb in range(b + 1):
            prob = parts[kb] * inverse
            PT[tile(b, kb)] = prob
            out = out + tn(prob.astype(bf16), two(VU, kb))
        OS[2 * b : 2 * b + 2] = out.astype(bf16).reshape(2, 192, 128)
        for s in (2 * b, 2 * b + 1):
            from_host(OS, OB, oh, oi, s)

    b_step(3)
    x_relay(-2)
    x_relay(2)
    a_step(1, 1)


    @pl.when(is_host)
    def _():
        arrived(KU, ki)
        arrived(QU, qi)
        arrived(VU, vi)
        for kb in range(blocks):
            KT[:, kb * BLOCK : (kb + 1) * BLOCK] = two(KU, kb).astype(f32).T.astype(bf16)
        for b in (0, 1):
            forward(b)

    arrived(PB(-4, 0), yb[-4])
    b_to_x(-4)
    x_relay(-3)
    x_relay(3)
    a_step(2, 0)


    @pl.when(is_host)
    def _():
        forward(2)

    back0 = (back0, sum_middle(0, back0, adapter_scale))
    x_relay(-4)
    a_step(2, 1)

    @pl.when(is_host)
    def _():
        forward(3)

    arrived(GB.at[across, half[0]], g_low_half)
    go(GB.at[across, half[0]], gs, g_rest, ctx, partner)
    arrived(GB.at[across, half[1]], g_high_half)
    go(GB.at[across, half[1]], gs, g_rest, ctx, partner)

    a_step(3, 0)
    a_step(3, 1)

    arrived(GB.at[pl.ds(0, 4)], g_rest)

    def a_part(d):
        yy = row(d)
        return nn(GB[yy], WA[yy].reshape(640, 256))

    total_a = a_part(0)
    for d in (-1, 1, -2, 2, -3, 3):
        total_a = total_a + a_part(d)
    arrived(OB, oi)
    mid0 = sum_start(1, nt(OB[...], down_full))
    lora_back = sum_end(0, back0[1])
    UPD[:, :, 0:512] = tn(lora_back, OB[...])[:64].reshape(8, 8, 512)
    total_a = total_a + nn(lora_back, down_full[:, :256])
    total_b = nn(lora_back, down_full[:, 256:])


    a_arrived(-4, 0)
    a_arrived(4, 1)
    total_a = total_a + a_part(4)
    DOB[:, 0:256] = total_a.astype(bf16)
    to_hosts(DOB, DU, di, ds, (0, 1))

    arrived(WB.at[pl.ds(0, 4)], xlast)
    for yy in range(8):
        total_b = total_b + nn(GB[yy], WB[yy].reshape(640, 256))
    DOB[:, 256:512] = total_b.astype(bf16)
    to_hosts(DOB, DU, di, ds, (2, 3))

    gq, gk, gv = [recv_id() for _ in range(3)]
    hq, hk, hv = [send_id() for _ in range(3)]

    def backward(b):
        grad, query = two(DU, b), two(QU, b)
        parts = []
        delta = jnp.zeros((1, BLOCK), f32)
        for kb in range(b + 1):
            part = nt(two(VU, kb), grad)
            delta = delta + jnp.sum(PT[tile(b, kb)] * part, axis=0, keepdims=True)
            parts.append(part)
        turned = jnp.zeros((128, BLOCK), f32)
        for kb in reversed(range(b + 1)):
            span = pl.ds(kb * BLOCK, BLOCK)
            prob = PT[tile(b, kb)]
            pull = (prob * (parts[kb] - delta) * scale).astype(bf16)
            key_part, value_part = nn(pull, query), nn(prob.astype(bf16), grad)
            if b < blocks - 1:
                key_part, value_part = DKA[span] + key_part, DVA[span] + value_part
            if kb == b:
                DKS[2 * b : 2 * b + 2] = key_part.astype(bf16).reshape(2, 192, 128)
                DVS[2 * b : 2 * b + 2] = value_part.astype(bf16).reshape(2, 192, 128)
                for s in (2 * b, 2 * b + 1):
                    from_host(DKS, dk_ref, hk, gk, s)
                    from_host(DVS, dv_ref, hv, gv, s)
            else:
                DKA[span], DVA[span] = key_part, value_part
            turned = turned + nn(KT[:, span], pull)
        DQS[2 * b : 2 * b + 2] = turned.T.astype(bf16).reshape(2, 192, 128)
        for s in (2 * b, 2 * b + 1):
            from_host(DQS, dq_ref, hq, gq, s)

    mid1 = sum_middle(1, mid0, 1.0)

    @pl.when(is_host)
    def _():
        arrived(DU, di)
        backward(3)

    lora_mid = sum_end(1, mid1)
    UPD[:, :, 512:1152] = (adapter_scale * tn(lora_mid, GB[f]))[:64].reshape(8, 8, 640)
    rs1_s, rs1_r = send_id(), recv_id()
    for j in range(1, 8):
        go(UPD.at[row(j)], rs1_s, rs1_r, ydev(j), f, R1.at[y])


    @pl.when(is_host)
    def _():
        backward(2)

    arrived(R1.at[pl.ds(0, 7)], rs1_r)
    total = UPD[y]
    for j in range(1, 8):
        total = total + R1[row(j)]
    for j in range(8):
        S2[j] = total[j : j + 1]
    rs2_s, rs2_r = send_id(), recv_id()
    for j in range(1, 8):
        to = (g + j) % 8
        go(S2.at[to], rs2_s, rs2_r, at(y, to), f, R2.at[g])


    @pl.when(is_host)
    def _():
        for b in (1, 0):
            backward(b)

    arrived(R2.at[pl.ds(0, 7)], rs2_r)
    total = S2[g]
    for j in range(1, 8):
        total = total + R2[(g + j) % 8]
    dn_ref[...] = total[:, 0:512]
    up_ref[...] = total[:, 512:1152]

    arrived(dq_ref, gq)
    arrived(dk_ref, gk)
    arrived(dv_ref, gv)

    seven = pl.ds(0, 7)
    left(WA.at[0, pl.ds(0, 6)], few)
    left(WB, all_b)
    left(WA.at[seven], all_a)
    left(GB.at[seven], gs)
    left(AD1.at[seven], ad1_s)
    left(AD2.at[seven], ad2_s)
    left(PSS.at[0, seven], back0[0][0])
    left(PSG.at[0, seven], back0[1][0])
    left(PSS.at[1, seven], mid0[0])
    left(PSG.at[1, seven], mid1[0])
    left(UPD.at[seven], rs1_s)
    left(S2.at[seven], rs2_s)

    @pl.when(is_host)
    def _():
        for send in to_host_sends:
            left(KU.at[pl.ds(0, 3)], send)
        for send in (oh, hq, hk, hv):
            left(OS.at[seven], send)

    @pl.when(jnp.logical_not(is_host))
    def _():
        for send in to_host_sends:
            left(KU.at[pl.ds(0, 4)], send)

    assert sent[0] <= SENDS and heard[0] <= RECVS, (sent, heard)


def finish_kernel(*refs):
    for src, dst in zip(refs[:5], refs[5:]):
        dst[...] = src[...]


def on_device(q, k, v, grad, codes, index, table, down, up):
    vmem = pl.BlockSpec(memory_space=pltpu.VMEM)
    tokens, width = q.shape
    out = jax.ShapeDtypeStruct((tokens, width), bf16)
    slabs = pltpu.VMEM((8, 192, 128), bf16)
    results = pl.pallas_call(
        kernel,
        name="block_backward",
        out_shape=(
            out,
            out,
            out,
            jax.ShapeDtypeStruct((1, width), f32),
            jax.ShapeDtypeStruct((1, grad.shape[1]), f32),
        ),
        in_specs=[vmem] * 5 + [pl.BlockSpec(memory_space=pl.ANY)] * 4,
        out_specs=[vmem] * 5,
        scratch_shapes=[
            pltpu.VMEM((8, 8, 80, 256), bf16),
            pltpu.VMEM((8, 8, 80, 256), bf16),
            pltpu.VMEM((8, 192, 640), bf16),
            slabs,
            slabs,
            slabs,
            slabs,
            pltpu.VMEM((10, BLOCK, BLOCK), f32),
            pltpu.VMEM((128, 1536), bf16),
            pltpu.VMEM((192, 512), bf16),
            slabs,
            slabs,
            slabs,
            slabs,
            pltpu.VMEM((1536, 128), f32),
            pltpu.VMEM((1536, 128), f32),
            pltpu.VMEM((192, 512), bf16),
            pltpu.VMEM((8, 1, 1152), f32),
            pltpu.VMEM((8, 8, 1152), f32),
            pltpu.VMEM((2, 8, 24, 128), f32),
            pltpu.VMEM((2, 8, 24, 128), f32),
            pltpu.VMEM((2, 8, 24, 128), f32),
            pltpu.VMEM((8, 8, 1152), f32),
            pltpu.VMEM((8, 8, 1152), f32),
            pltpu.VMEM((8, 1, 1152), f32),
            pltpu.VMEM((8, 1, 1152), f32),
            pltpu.SemaphoreType.DMA((SENDS,)),
            pltpu.SemaphoreType.DMA((RECVS,)),
            pltpu.SemaphoreType.DMA((1,)),
        ],
        compiler_params=pltpu.CompilerParams(
            collective_id=0, has_side_effects=True, vmem_limit_bytes=56 * 1024 * 1024
        ),
    )(codes, index.T, table.reshape(1, -1), down, up, q, k, v, grad)
    return pl.pallas_call(
        finish_kernel,
        name="finish",
        out_shape=tuple(jax.ShapeDtypeStruct(r.shape, r.dtype) for r in results),
        in_specs=[vmem] * 5,
        out_specs=[vmem] * 5,
    )(*results)


def solution(mesh):
    spec = P("ctx", "fsdp")
    return jax.shard_map(
        on_device,
        mesh=mesh,
        in_specs=(spec, spec, spec, spec, spec, spec, P(), spec, spec),
        out_specs=(spec,) * 5,
        check_vma=False,
    )
```

```python
import jax
import jax.numpy as jnp
from jax import lax
from jax.experimental import pallas as pl
from jax.experimental.pallas import tpu as pltpu
from jax.sharding import PartitionSpec as P

HEAD_WIDTH = 128
MESH = pl.DeviceIdType.MESH
BLOCK = 384
nf4_values = (
    -1.0,
    -0.6961928009986877,
    -0.5250730514526367,
    -0.39491748809814453,
    -0.28444138169288635,
    -0.18477343022823334,
    -0.09105003625154495,
    0.0,
    0.07958029955625534,
    0.16093020141124725,
    0.24611230194568634,
    0.33791524171829224,
    0.44070982933044434,
    0.5626170039176941,
    0.7229568362236023,
    1.0,
)
adapter_scale = 0.25
masked = -1e30
f32, bf16 = jnp.float32, jnp.bfloat16
SENDS, RECVS = 24, 72


def nt(a, b):
    return lax.dot_general(a, b, (((1,), (1,)), ((), ())), preferred_element_type=f32)


def tn(a, b):
    return lax.dot_general(a, b, (((0,), (0,)), ((), ())), preferred_element_type=f32)


def nn(a, b):
    return jnp.dot(a, b, preferred_element_type=f32)


def kernel(
    codes_hbm, index_hbm, table_hbm, ad_hbm, au_hbm, q_ref, k_ref, v_ref, g_ref,
    dq_ref, dk_ref, dv_ref, dn_ref, up_ref,
    WA, WB, GB, QU, KU, VU, DU, PT, KT, OB, OS, DQS, DKS, DVS, DKA, DVA, DOB,
    AD1, AD2, PSS, PSR, PSG, UPD, R1, S2, R2, CODES, INDEX, TABLE, DOWN, UP, ss, rs, ls,
):
    ctx = lax.axis_index("ctx")
    f = lax.axis_index("fsdp")
    y, g = ctx // 8, ctx % 8
    x, zl = g // 2, g % 2
    c = f % 2
    partner = f + 1 - 2 * c
    scale = HEAD_WIDTH ** (-0.5)
    shifted_x = 3 * (1 - c)
    shifted_host = x == shifted_x
    is_host = jnp.logical_or(x == 1 + c, shifted_host)
    unit_head = jnp.where(shifted_host, 2, 0) + zl


    sent, heard = [0], [0]

    def send_id():
        sent[0] += 1
        return sent[0] - 1

    def recv_id():
        heard[0] += 1
        return heard[0] - 1

    def remote(src, dst, send, recv, to_ctx, to_f):
        return pltpu.make_async_remote_copy(
            src_ref=src,
            dst_ref=dst,
            send_sem=ss.at[send],
            recv_sem=rs.at[recv],
            device_id={"ctx": to_ctx, "fsdp": to_f},
            device_id_type=MESH,
        )

    def go(src, send, recv, to_ctx, to_f, dst=None):
        remote(src, src if dst is None else dst, send, recv, to_ctx, to_f).start()

    def arrived(dst, recv):
        pltpu.make_async_copy(dst, dst, rs.at[recv]).wait()

    def left(src, send):
        pltpu.make_async_copy(src, src, ss.at[send]).wait()

    def row(dy):
        return (y + dy) % 8

    def at(yy, gg):
        return yy * 8 + gg

    def ydev(dy):
        return at(row(dy), g)

    def xdev(dx):
        return at(y, ((x + dx) % 4) * 2 + zl)

    def fdev(df):
        return (f + df) % 8

    other_row = jnp.where(x < 2, (y + 7) % 8, (y + 1) % 8)
    other_g = jnp.where(x < 2, 4, 0)

    barrier = pltpu.get_barrier_semaphore()
    peers = [(at(y, (g + j) % 8), f) for j in range(1, 8)]
    peers += [(ydev(j), f) for j in range(1, 8)]
    peers += [(ctx, fdev(j)) for j in range(1, 8)]
    peers += [(at(other_row, other_g + j), f) for j in range(4)]
    for to_ctx, to_f in peers:
        pl.semaphore_signal(
            barrier, inc=1, device_id={"ctx": to_ctx, "fsdp": to_f}, device_id_type=MESH
        )
    own_grad = pltpu.make_async_copy(g_ref, GB.at[f], ls.at[0])
    loads = [
        pltpu.make_async_copy(src, dst, ls.at[n + 1])
        for n, (src, dst) in enumerate(
            (
                (codes_hbm, CODES),
                (index_hbm, INDEX),
                (table_hbm, TABLE),
                (ad_hbm, DOWN),
                (au_hbm, UP),
            )
        )
    ]
    for copy in loads:
        copy.start()
    own_grad.start()
    for copy in loads:
        copy.wait()

    codes = CODES[...]
    values = jnp.zeros(codes.shape, f32)
    for level in range(16):
        values = jnp.where(codes == level, nf4_values[level], values)
    table = TABLE[...]
    index = jnp.concatenate([INDEX[...].astype(f32), jnp.zeros((8, 48), f32)], axis=1)
    index = index.T[: codes.shape[0]].astype(jnp.int32)
    level_at = lax.broadcasted_iota(jnp.int32, (codes.shape[0], table.shape[1]), 1)
    block_at = lax.broadcasted_iota(jnp.int32, codes.shape, 1) // 64
    scales = jnp.zeros(codes.shape, f32)
    for block in range(8):
        picked = jnp.where(index[:, block : block + 1] == level_at, table, 0.0)
        picked = jnp.sum(picked, axis=1, keepdims=True)
        scales = jnp.where(block_at == block, picked, scales)
    weight = (values * scales).astype(bf16)
    WA[y, g] = weight[:, :256]
    WB[y, g] = weight[:, 256:]
    AD1[y] = jnp.concatenate([DOWN[...].astype(f32), UP[...].astype(f32)], axis=1)
    pl.semaphore_wait(barrier, len(peers))

    pair = ctx + 1 - 2 * zl
    first, few = recv_id(), send_id()
    go(WA.at[y, g], few, first, pair, f)
    go(WB.at[y, g], few, first, pair, f)

    ad1_s, ad1_r = send_id(), recv_id()
    for j in range(1, 8):
        go(AD1.at[y], ad1_s, ad1_r, ydev(j), f)

    def PB(dy, dx):
        return WB.at[row(dy), pl.ds(((x + dx) % 4) * 2, 2)]

    def QA(dy, dx):
        return WA.at[row(dy), pl.ds(((x + dx) % 4) * 2, 2)]

    up_relay = (-1, 0, 1)
    yb = {d: recv_id() for d in (-4, -3, -2, -1, 1, 2, 3)}
    xlast = recv_id()
    xb = {}
    for d in range(-4, 4):
        xb[(-1, d)] = recv_id() if d in up_relay else xlast
        xb[(1, d)] = xlast if d in up_relay else recv_id()
    all_b, all_a = send_id(), send_id()

    def b_to_x(d):
        go(PB(d, 0), all_b, xb[(-1, d)], xdev(1), f)
        go(PB(d, 0), all_b, xb[(1, d)], xdev(-1), f)

    def b_up(d):
        go(PB(d, 0), all_b, yb[d - 1], ydev(1), f)

    def b_down(d):
        go(PB(d, 0), all_b, yb[d + 1], ydev(-1), f)

    def x_relay(d):
        side = -1 if d in up_relay else 1
        arrived(PB(d, side), xb[(side, d)])
        go(PB(d, side), all_b, xlast, xdev(-side), f)

    around = (0, -1, 1, 2)
    ya = {(d, dx): recv_id() for d in (-3, -2, -1, 1, 2, 3) for dx in around}
    for d, dx in ((-4, 0), (-4, -1), (4, 1), (4, 2)):
        ya[(d, dx)] = recv_id()

    def a_up(d, dx):
        go(QA(d, dx), all_a, ya[(d - 1, dx)], ydev(1), f)

    def a_down(d, dx):
        go(QA(d, dx), all_a, ya[(d + 1, dx)], ydev(-1), f)

    def a_arrived(d, dx):
        arrived(QA(d, dx), ya[(d, dx)])

    def a_step(d, dx):
        a_arrived(-d, dx)
        if d < 3 or dx in (0, -1):
            a_up(-d, dx)
        a_arrived(d, dx)
        if d < 3 or dx in (1, 2):
            a_down(d, dx)

    def b_step(d):
        arrived(PB(-d, 0), yb[-d])
        b_up(-d)
        b_to_x(-d)
        arrived(PB(d, 0), yb[d])
        if d < 3:
            b_down(d)
        b_to_x(d)

    xa = {dx: recv_id() for dx in (-1, 1, 2)}

    def spread(z):
        block_a, block_b = WA.at[y, 2 * x + z], WB.at[y, 2 * x + z]
        for up in (1, -1):
            go(block_b, all_b, yb[-up], ydev(up), f)
            go(block_a, few, xa[-up], xdev(up), f)
            go(block_b, all_b, xb[(-up, 0)], xdev(up), f)
            go(block_a, all_a, ya[(-up, 0)], ydev(up), f)

    spread(zl)
    arrived(WA.at[0, pl.ds(0, 2)], first)
    spread(1 - zl)

    half = [pl.ds(0, 96), pl.ds(96, 96)]
    gs = send_id()
    g_own, g_low, g_high, g_low_half, g_high_half, g_rest = [recv_id() for _ in range(6)]
    own_grad.wait()
    go(GB.at[f], gs, g_low, ctx, fdev(2))
    go(GB.at[f], gs, g_high, ctx, fdev(6))
    go(GB.at[f], gs, g_rest, ctx, partner)

    def slab_of(head):
        return g if head < 2 else (g + 4) % 8

    def host_of(head):
        if head < 2:
            return at(y, (1 + c) * 2 + head)
        first_row = jnp.where(x < 2, (y + 7) % 8, y)
        return at((first_row + c) % 8, shifted_x * 2 + head - 2)

    to_host_sends = []

    def to_hosts(src_ref, dst_buf, recv, send, heads):
        for head in heads:
            dest = host_of(head)
            slot = slab_of(head)
            src = src_ref.at[:, head * 128 : (head + 1) * 128]
            dst = dst_buf.at[slot]
            away = dest != ctx

            @pl.when(away)
            def _():
                go(src, send, recv, dest, f, dst)

            @pl.when(jnp.logical_not(away))
            def _():
                pltpu.make_async_copy(src, dst, rs.at[recv]).start()

    ki, qi, vi, di = [recv_id() for _ in range(4)]
    ks, qs, vs, ds = to_host_sends = [send_id() for _ in range(4)]

    def slabs():
        to_hosts(k_ref, KU, ki, ks, range(4))
        to_hosts(q_ref, QU, qi, qs, range(4))
        to_hosts(v_ref, VU, vi, vs, range(4))

    for dx in (-1, 1):
        arrived(QA(0, dx), xa[dx])
        if dx == -1:
            part = WA.at[y, ((x + 3) % 4) * 2]
            go(part, all_b, xa[2], xdev(1), f)
        else:
            part = WA.at[y, ((x + 1) % 4) * 2 + 1]
            go(part, all_b, xa[2], xdev(-1), f)
    b_step(1)
    for dx in (-1, 1):
        a_up(0, dx)
        a_down(0, dx)
    slabs()
    arrived(AD1.at[pl.ds(0, 7)], ad1_r)
    AD2[g] = jnp.concatenate([AD1[j] for j in range(8)], axis=0).astype(bf16)
    ad2_s, ad2_r = send_id(), recv_id()
    for j in range(1, 8):
        go(AD2.at[g], ad2_s, ad2_r, at(y, (g + j) % 8), f)

    arrived(QA(0, 2), xa[2])
    a_up(0, 2)
    a_down(0, 2)
    b_step(2)
    a_step(1, 0)
    a_step(1, -1)
    first_row = (y + 8 - c) % 8

    def source_of(slot):
        if slot < 4:
            return jnp.where(shifted_host, at(first_row, slot + 4), at(y, slot))
        return jnp.where(shifted_host, at((first_row + 1) % 8, slot - 4), at(y, slot))

    head_columns = pl.ds(pl.multiple_of(unit_head * 128, 128), 128)

    def from_host(buf, dst_ref, send, recv, slot):
        dest = source_of(slot)
        src, dst = buf.at[slot], dst_ref.at[:, head_columns]
        away = dest != ctx

        @pl.when(away)
        def _():
            go(src, send, recv, dest, f, dst)

        @pl.when(jnp.logical_not(away))
        def _():
            pltpu.make_async_copy(src, dst, rs.at[recv]).start()

    blocks = 1536 // BLOCK

    def two(buf, b):
        return buf[2 * b : 2 * b + 2].reshape(BLOCK, 128)

    def tile(b, kb):
        return b * (b + 1) // 2 + kb

    oh, oi = send_id(), recv_id()

    def forward(b):
        key_at = lax.broadcasted_iota(jnp.int32, (BLOCK, BLOCK), 0)
        query_at = lax.broadcasted_iota(jnp.int32, (BLOCK, BLOCK), 1)
        seen = key_at <= query_at
        query = two(QU, b)
        parts = []
        for kb in range(b + 1):
            part = nt(two(KU, kb), query) * scale
            parts.append(jnp.where(seen, part, masked) if kb == b else part)
        top = jnp.max(parts[0], axis=0, keepdims=True)
        for part in parts[1:]:
            top = jnp.maximum(top, jnp.max(part, axis=0, keepdims=True))
        parts = [jnp.exp(part - top) for part in parts]
        total = jnp.sum(parts[0], axis=0, keepdims=True)
        for part in parts[1:]:
            total = total + jnp.sum(part, axis=0, keepdims=True)
        inverse = 1.0 / total
        out = jnp.zeros((BLOCK, 128), f32)
        for kb in range(b + 1):
            prob = parts[kb] * inverse
            PT[tile(b, kb)] = prob
            out = out + tn(prob.astype(bf16), two(VU, kb))
        OS[2 * b : 2 * b + 2] = out.astype(bf16).reshape(2, 192, 128)
        for s in (2 * b, 2 * b + 1):
            from_host(OS, OB, oh, oi, s)

    def sum_start(n, piece):
        PSS[n] = piece.reshape(8, 24, 128)
        send, recv = send_id(), recv_id()
        for j in range(1, 8):
            to = fdev(j)
            go(PSS.at[n, to], send, recv, ctx, to, PSR.at[n, f])
        return send, recv

    def sum_middle(n, pair, factor):
        arrived(PSR.at[n, pl.ds(0, 7)], pair[1])
        total = PSS[n, f]
        for j in range(1, 8):
            total = total + PSR[n, fdev(j)]
        PSG[n, f] = (total * factor).astype(bf16).astype(f32)
        send, recv = send_id(), recv_id()
        for j in range(1, 8):
            go(PSG.at[n, f], send, recv, ctx, fdev(j))
        return send, recv

    def sum_end(n, pair):
        arrived(PSG.at[n, pl.ds(0, 7)], pair[1])
        return PSG[n].reshape(192, 128).astype(bf16)

    b_step(3)
    a_step(1, 1)
    a_step(1, 2)
    x_relay(0)

    below, above, across = fdev(6), fdev(2), fdev(4)
    arrived(GB.at[below], g_low)
    go(GB.at[below, half[0]], gs, g_low_half, ctx, above)
    go(GB.at[below], gs, g_rest, ctx, partner)
    arrived(GB.at[above], g_high)
    go(GB.at[above, half[1]], gs, g_high_half, ctx, below)
    go(GB.at[above], gs, g_rest, ctx, partner)


    @pl.when(is_host)
    def _():
        arrived(KU, ki)
        arrived(QU, qi)
        arrived(VU, vi)
        for kb in range(blocks):
            KT[:, kb * BLOCK : (kb + 1) * BLOCK] = two(KU, kb).astype(f32).T.astype(bf16)
        for b in (0, 1):
            forward(b)

    arrived(PB(-4, 0), yb[-4])
    b_to_x(-4)
    a_step(2, 0)
    a_step(2, -1)
    x_relay(-1)
    x_relay(1)
    arrived(AD2.at[pl.ds(0, 7)], ad2_r)
    adapters = AD2[...].astype(f32).reshape(64, 1152).astype(bf16)
    adapters = jnp.concatenate([adapters, jnp.zeros_like(adapters)], axis=0)
    down_full, up_piece = adapters[:, :512], adapters[:, 512:]
    back0 = sum_start(0, nt(GB[f], up_piece))


    @pl.when(is_host)
    def _():
        forward(2)

    a_step(2, 1)
    a_step(2, 2)
    x_relay(-2)
    x_relay(2)

    @pl.when(is_host)
    def _():
        forward(3)

    a_step(3, 0)
    a_step(3, -1)
    x_relay(-3)
    x_relay(3)

    back0 = (back0, sum_middle(0, back0, adapter_scale))
    a_step(3, 1)
    a_step(3, 2)

    x_relay(-4)
    arrived(GB.at[across, half[0]], g_low_half)
    go(GB.at[across, half[0]], gs, g_rest, ctx, partner)
    arrived(GB.at[across, half[1]], g_high_half)
    go(GB.at[across, half[1]], gs, g_rest, ctx, partner)

    arrived(OB, oi)
    mid0 = sum_start(1, nt(OB[...], down_full))
    arrived(GB.at[pl.ds(0, 4)], g_rest)

    def a_part(d):
        yy = row(d)
        return nn(GB[yy], WA[yy].reshape(640, 256))

    total_a = a_part(0)
    for d in (-1, 1, -2, 2, -3, 3):
        total_a = total_a + a_part(d)
    lora_back = sum_end(0, back0[1])
    UPD[:, :, 0:512] = tn(lora_back, OB[...])[:64].reshape(8, 8, 512)
    rs0_s, rs0_r = send_id(), recv_id()
    for j in range(1, 8):
        to = (g + j) % 8
        go(UPD.at[to, :, 0:512], rs0_s, rs0_r, at(y, to), f, R1.at[g, :, 0:512])
    total_a = total_a + nn(lora_back, down_full[:, :256])
    total_b = nn(lora_back, down_full[:, 256:])


    arrived(WB.at[pl.ds(0, 4)], xlast)
    for yy in range(8):
        total_b = total_b + nn(GB[yy], WB[yy].reshape(640, 256))
    DOB[:, 256:512] = total_b.astype(bf16)
    to_hosts(DOB, DU, di, ds, (2, 3))

    for d, dx in ((-4, 0), (-4, -1), (4, 1), (4, 2)):
        a_arrived(d, dx)
    total_a = total_a + a_part(4)
    DOB[:, 0:256] = total_a.astype(bf16)
    to_hosts(DOB, DU, di, ds, (0, 1))

    gq, gk, gv = [recv_id() for _ in range(3)]
    hq, hk, hv = [send_id() for _ in range(3)]

    def backward(b):
        grad, query = two(DU, b), two(QU, b)
        parts = []
        delta = jnp.zeros((1, BLOCK), f32)
        for kb in range(b + 1):
            part = nt(two(VU, kb), grad)
            delta = delta + jnp.sum(PT[tile(b, kb)] * part, axis=0, keepdims=True)
            parts.append(part)
        turned = jnp.zeros((128, BLOCK), f32)
        for kb in reversed(range(b + 1)):
            span = pl.ds(kb * BLOCK, BLOCK)
            prob = PT[tile(b, kb)]
            pull = (prob * (parts[kb] - delta) * scale).astype(bf16)
            key_part, value_part = nn(pull, query), nn(prob.astype(bf16), grad)
            if b < blocks - 1:
                key_part, value_part = DKA[span] + key_part, DVA[span] + value_part
            if kb == b:
                DKS[2 * b : 2 * b + 2] = key_part.astype(bf16).reshape(2, 192, 128)
                DVS[2 * b : 2 * b + 2] = value_part.astype(bf16).reshape(2, 192, 128)
                for s in (2 * b, 2 * b + 1):
                    from_host(DKS, dk_ref, hk, gk, s)
                    from_host(DVS, dv_ref, hv, gv, s)
            else:
                DKA[span], DVA[span] = key_part, value_part
            turned = turned + nn(KT[:, span], pull)
        DQS[2 * b : 2 * b + 2] = turned.T.astype(bf16).reshape(2, 192, 128)
        for s in (2 * b, 2 * b + 1):
            from_host(DQS, dq_ref, hq, gq, s)

    mid1 = sum_middle(1, mid0, 1.0)

    @pl.when(is_host)
    def _():
        arrived(DU, di)
        backward(3)

    lora_mid = sum_end(1, mid1)
    UPD[:, :, 512:1152] = (adapter_scale * tn(lora_mid, GB[f]))[:64].reshape(8, 8, 640)
    rs1_s, rs1_r = send_id(), recv_id()
    for j in range(1, 8):
        to = (g + j) % 8
        go(UPD.at[to, :, 512:1152], rs1_s, rs1_r, at(y, to), f, R1.at[g, :, 512:1152])


    @pl.when(is_host)
    def _():
        for b in (2, 1, 0):
            backward(b)

    arrived(R1.at[pl.ds(0, 7), :, 0:512], rs0_r)
    arrived(R1.at[pl.ds(0, 7), :, 512:1152], rs1_r)
    total = UPD[g]
    for j in range(1, 8):
        total = total + R1[(g + j) % 8]
    for j in range(8):
        S2[j] = total[j : j + 1]
    rs2_s, rs2_r = send_id(), recv_id()
    for j in range(1, 8):
        go(S2.at[row(j)], rs2_s, rs2_r, ydev(j), f, R2.at[y])

    arrived(R2.at[pl.ds(0, 7)], rs2_r)
    total = S2[y]
    for j in range(1, 8):
        total = total + R2[row(j)]
    dn_ref[...] = total[:, 0:512]
    up_ref[...] = total[:, 512:1152]

    arrived(dq_ref, gq)
    arrived(dk_ref, gk)
    arrived(dv_ref, gv)

    seven = pl.ds(0, 7)
    left(WA.at[0, pl.ds(0, 6)], few)
    left(WB, all_b)
    left(WA.at[seven], all_a)
    left(GB.at[seven], gs)
    left(AD1.at[seven], ad1_s)
    left(AD2.at[seven], ad2_s)
    left(PSS.at[0, seven], back0[0][0])
    left(PSG.at[0, seven], back0[1][0])
    left(PSS.at[1, seven], mid0[0])
    left(PSG.at[1, seven], mid1[0])
    left(UPD.at[seven, :, 0:512], rs0_s)
    left(UPD.at[seven, :, 512:1152], rs1_s)
    left(S2.at[seven], rs2_s)

    @pl.when(is_host)
    def _():
        for send in to_host_sends:
            left(KU.at[pl.ds(0, 3)], send)
        for send in (oh, hq, hk, hv):
            left(OS.at[seven], send)

    @pl.when(jnp.logical_not(is_host))
    def _():
        for send in to_host_sends:
            left(KU.at[pl.ds(0, 4)], send)

    assert sent[0] <= SENDS and heard[0] <= RECVS, (sent, heard)


def finish_kernel(*refs):
    copies = [pltpu.make_async_copy(refs[n], refs[5 + n], refs[10].at[n]) for n in range(5)]
    for copy in copies:
        copy.start()
    for copy in copies:
        copy.wait()


def on_device(q, k, v, grad, codes, index, table, down, up):
    vmem = pl.BlockSpec(memory_space=pltpu.VMEM)
    tokens, width = q.shape
    out = jax.ShapeDtypeStruct((tokens, width), bf16)
    slabs = pltpu.VMEM((8, 192, 128), bf16)
    results = pl.pallas_call(
        kernel,
        name="block_backward",
        out_shape=(
            out,
            out,
            out,
            jax.ShapeDtypeStruct((1, width), f32),
            jax.ShapeDtypeStruct((1, grad.shape[1]), f32),
        ),
        in_specs=[pl.BlockSpec(memory_space=pl.ANY)] * 9,
        out_specs=[vmem] * 5,
        scratch_shapes=[
            pltpu.VMEM((8, 8, 80, 256), bf16),
            pltpu.VMEM((8, 8, 80, 256), bf16),
            pltpu.VMEM((8, 192, 640), bf16),
            slabs,
            slabs,
            slabs,
            slabs,
            pltpu.VMEM((10, BLOCK, BLOCK), f32),
            pltpu.VMEM((128, 1536), bf16),
            pltpu.VMEM((192, 512), bf16),
            slabs,
            slabs,
            slabs,
            slabs,
            pltpu.VMEM((1536, 128), f32),
            pltpu.VMEM((1536, 128), f32),
            pltpu.VMEM((192, 512), bf16),
            pltpu.VMEM((8, 1, 1152), f32),
            pltpu.VMEM((8, 8, 1152), bf16),
            pltpu.VMEM((2, 8, 24, 128), f32),
            pltpu.VMEM((2, 8, 24, 128), f32),
            pltpu.VMEM((2, 8, 24, 128), f32),
            pltpu.VMEM((8, 8, 1152), f32),
            pltpu.VMEM((8, 8, 1152), f32),
            pltpu.VMEM((8, 1, 1152), f32),
            pltpu.VMEM((8, 1, 1152), f32),
            pltpu.VMEM(codes.shape, jnp.int32),
            pltpu.VMEM(index.shape[::-1], jnp.int32),
            pltpu.VMEM((1, table.shape[0]), f32),
            pltpu.VMEM(down.shape, bf16),
            pltpu.VMEM(up.shape, bf16),
            pltpu.SemaphoreType.DMA((SENDS,)),
            pltpu.SemaphoreType.DMA((RECVS,)),
            pltpu.SemaphoreType.DMA((6,)),
        ],
        compiler_params=pltpu.CompilerParams(
            collective_id=0, has_side_effects=True, vmem_limit_bytes=56 * 1024 * 1024
        ),
    )(codes, index.T, table.reshape(1, -1), down, up, q, k, v, grad)
    return pl.pallas_call(
        finish_kernel,
        name="finish",
        out_shape=tuple(jax.ShapeDtypeStruct(r.shape, r.dtype) for r in results),
        in_specs=[vmem] * 5,
        out_specs=[pl.BlockSpec(memory_space=pl.ANY)] * 5,
        scratch_shapes=[pltpu.SemaphoreType.DMA((5,))],
    )(*results)


def solution(mesh):
    spec = P("ctx", "fsdp")
    return jax.shard_map(
        on_device,
        mesh=mesh,
        in_specs=(spec, spec, spec, spec, spec, spec, P(), spec, spec),
        out_specs=(spec,) * 5,
        check_vma=False,
    )
```

```python
import jax
import jax.numpy as jnp
from jax import lax
from jax.experimental import pallas as pl
from jax.experimental.pallas import tpu as pltpu
from jax.sharding import PartitionSpec as P

HEAD_WIDTH = 128
MESH = pl.DeviceIdType.MESH
BLOCK = 384
nf4_values = (
    -1.0,
    -0.6961928009986877,
    -0.5250730514526367,
    -0.39491748809814453,
    -0.28444138169288635,
    -0.18477343022823334,
    -0.09105003625154495,
    0.0,
    0.07958029955625534,
    0.16093020141124725,
    0.24611230194568634,
    0.33791524171829224,
    0.44070982933044434,
    0.5626170039176941,
    0.7229568362236023,
    1.0,
)
adapter_scale = 0.25
masked = -1e30
f32, bf16 = jnp.float32, jnp.bfloat16
SENDS, RECVS = 24, 72


def nt(a, b):
    return lax.dot_general(a, b, (((1,), (1,)), ((), ())), preferred_element_type=f32)


def tn(a, b):
    return lax.dot_general(a, b, (((0,), (0,)), ((), ())), preferred_element_type=f32)


def nn(a, b):
    return jnp.dot(a, b, preferred_element_type=f32)


def kernel(
    codes_hbm, index_hbm, table_hbm, ad_hbm, au_hbm, q_ref, k_ref, v_ref, g_ref,
    dq_ref, dk_ref, dv_ref, dn_ref, up_ref,
    WA, WB, GB, QU, KU, VU, DU, PT, KT, OB, OS, DQS, DKS, DVS, DKA, DVA, DOB,
    AD1, AD2, PS, UPD, R1, S2, R2, CODES, INDEX, TABLE, DOWN, UP, ss, rs, ls,
):
    ctx = lax.axis_index("ctx")
    f = lax.axis_index("fsdp")
    y, g = ctx // 8, ctx % 8
    x, zl = g // 2, g % 2
    c = f % 2
    partner = f + 1 - 2 * c
    scale = HEAD_WIDTH ** (-0.5)
    shifted_x = 3 * (1 - c)
    shifted_host = x == shifted_x
    is_host = jnp.logical_or(x == 1 + c, shifted_host)
    unit_head = jnp.where(shifted_host, 2, 0) + zl


    sent, heard = [0], [0]

    def send_id():
        sent[0] += 1
        return sent[0] - 1

    def recv_id():
        heard[0] += 1
        return heard[0] - 1

    def remote(src, dst, send, recv, to_ctx, to_f):
        return pltpu.make_async_remote_copy(
            src_ref=src,
            dst_ref=dst,
            send_sem=ss.at[send],
            recv_sem=rs.at[recv],
            device_id={"ctx": to_ctx, "fsdp": to_f},
            device_id_type=MESH,
        )

    def go(src, send, recv, to_ctx, to_f, dst=None):
        remote(src, src if dst is None else dst, send, recv, to_ctx, to_f).start()

    def arrived(dst, recv):
        pltpu.make_async_copy(dst, dst, rs.at[recv]).wait()

    def left(src, send):
        pltpu.make_async_copy(src, src, ss.at[send]).wait()

    def row(dy):
        return (y + dy) % 8

    def at(yy, gg):
        return yy * 8 + gg

    def ydev(dy):
        return at(row(dy), g)

    def xdev(dx):
        return at(y, ((x + dx) % 4) * 2 + zl)

    def fdev(df):
        return (f + df) % 8

    other_row = jnp.where(x < 2, (y + 7) % 8, (y + 1) % 8)
    other_g = jnp.where(x < 2, 4, 0)

    barrier = pltpu.get_barrier_semaphore()
    peers = [(at(y, (g + j) % 8), f) for j in range(1, 8)]
    peers += [(ydev(j), f) for j in range(1, 8)]
    peers += [(ctx, fdev(j)) for j in range(1, 8)]
    peers += [(at(other_row, other_g + j), f) for j in range(4)]
    for to_ctx, to_f in peers:
        pl.semaphore_signal(
            barrier, inc=1, device_id={"ctx": to_ctx, "fsdp": to_f}, device_id_type=MESH
        )
    own_grad = pltpu.make_async_copy(g_ref, GB.at[f], ls.at[0])
    loads = [
        pltpu.make_async_copy(src, dst, ls.at[n + 1])
        for n, (src, dst) in enumerate(
            (
                (codes_hbm, CODES),
                (index_hbm, INDEX),
                (table_hbm, TABLE),
                (ad_hbm, DOWN),
                (au_hbm, UP),
            )
        )
    ]
    for copy in loads:
        copy.start()
    own_grad.start()
    for copy in loads:
        copy.wait()

    codes = CODES[...]
    values = jnp.zeros(codes.shape, f32)
    for level in range(16):
        values = jnp.where(codes == level, nf4_values[level], values)
    table = TABLE[...]
    index = jnp.concatenate([INDEX[...].astype(f32), jnp.zeros((8, 48), f32)], axis=1)
    index = index.T[: codes.shape[0]].astype(jnp.int32)
    level_at = lax.broadcasted_iota(jnp.int32, (codes.shape[0], table.shape[1]), 1)
    block_at = lax.broadcasted_iota(jnp.int32, codes.shape, 1) // 64
    scales = jnp.zeros(codes.shape, f32)
    for block in range(8):
        picked = jnp.where(index[:, block : block + 1] == level_at, table, 0.0)
        picked = jnp.sum(picked, axis=1, keepdims=True)
        scales = jnp.where(block_at == block, picked, scales)
    weight = (values * scales).astype(bf16)
    WA[y, g] = weight[:, :256]
    WB[y, g] = weight[:, 256:]
    AD1[y] = jnp.concatenate([DOWN[...].astype(f32), UP[...].astype(f32)], axis=1)
    pl.semaphore_wait(barrier, len(peers))

    pair = ctx + 1 - 2 * zl
    first, few = recv_id(), send_id()
    go(WA.at[y, g], few, first, pair, f)
    go(WB.at[y, g], few, first, pair, f)

    ad1_s, ad1_r = send_id(), recv_id()
    for j in range(1, 8):
        go(AD1.at[y], ad1_s, ad1_r, ydev(j), f)

    def PB(dy, dx):
        return WB.at[row(dy), pl.ds(((x + dx) % 4) * 2, 2)]

    def QA(dy, dx):
        return WA.at[row(dy), pl.ds(((x + dx) % 4) * 2, 2)]

    up_relay = (-1, 0, 1)
    yb = {d: recv_id() for d in (-4, -3, -2, -1, 1, 2, 3)}
    xlast = recv_id()
    xb = {}
    for d in range(-4, 4):
        xb[(-1, d)] = recv_id() if d in up_relay else xlast
        xb[(1, d)] = xlast if d in up_relay else recv_id()
    all_b, all_a = send_id(), send_id()

    def b_to_x(d):
        go(PB(d, 0), all_b, xb[(-1, d)], xdev(1), f)
        go(PB(d, 0), all_b, xb[(1, d)], xdev(-1), f)

    def b_up(d):
        go(PB(d, 0), all_b, yb[d - 1], ydev(1), f)

    def b_down(d):
        go(PB(d, 0), all_b, yb[d + 1], ydev(-1), f)

    def x_relay(d):
        side = -1 if d in up_relay else 1
        arrived(PB(d, side), xb[(side, d)])
        go(PB(d, side), all_b, xlast, xdev(-side), f)

    around = (0, -1, 1, 2)
    ya = {(d, dx): recv_id() for d in (-3, -2, -1, 1, 2, 3) for dx in around}
    for d, dx in ((-4, 0), (-4, -1), (4, 1), (4, 2)):
        ya[(d, dx)] = recv_id()

    def a_up(d, dx):
        go(QA(d, dx), all_a, ya[(d - 1, dx)], ydev(1), f)

    def a_down(d, dx):
        go(QA(d, dx), all_a, ya[(d + 1, dx)], ydev(-1), f)

    def a_arrived(d, dx):
        arrived(QA(d, dx), ya[(d, dx)])

    def a_step(d, dx):
        a_arrived(-d, dx)
        if d < 3 or dx in (0, -1):
            a_up(-d, dx)
        a_arrived(d, dx)
        if d < 3 or dx in (1, 2):
            a_down(d, dx)

    def b_step(d):
        arrived(PB(-d, 0), yb[-d])
        b_up(-d)
        b_to_x(-d)
        arrived(PB(d, 0), yb[d])
        if d < 3:
            b_down(d)
        b_to_x(d)

    xa = {dx: recv_id() for dx in (-1, 1, 2)}

    def spread(z):
        block_a, block_b = WA.at[y, 2 * x + z], WB.at[y, 2 * x + z]
        for up in (1, -1):
            go(block_b, all_b, yb[-up], ydev(up), f)
            go(block_a, few, xa[-up], xdev(up), f)
            go(block_b, all_b, xb[(-up, 0)], xdev(up), f)
            go(block_a, all_a, ya[(-up, 0)], ydev(up), f)

    spread(zl)
    arrived(WA.at[0, pl.ds(0, 2)], first)
    spread(1 - zl)

    half = [pl.ds(0, 96), pl.ds(96, 96)]
    gs = send_id()
    g_own, g_low, g_high, g_low_half, g_high_half, g_rest = [recv_id() for _ in range(6)]
    own_grad.wait()
    go(GB.at[f], gs, g_low, ctx, fdev(2))
    go(GB.at[f], gs, g_high, ctx, fdev(6))
    go(GB.at[f], gs, g_rest, ctx, partner)

    def slab_of(head):
        return g if head < 2 else (g + 4) % 8

    def host_of(head):
        if head < 2:
            return at(y, (1 + c) * 2 + head)
        first_row = jnp.where(x < 2, (y + 7) % 8, y)
        return at((first_row + c) % 8, shifted_x * 2 + head - 2)

    to_host_sends = []

    def to_hosts(src_ref, dst_buf, recv, send, heads):
        for head in heads:
            dest = host_of(head)
            slot = slab_of(head)
            src = src_ref.at[:, head * 128 : (head + 1) * 128]
            dst = dst_buf.at[slot]
            away = dest != ctx

            @pl.when(away)
            def _():
                go(src, send, recv, dest, f, dst)

            @pl.when(jnp.logical_not(away))
            def _():
                pltpu.make_async_copy(src, dst, rs.at[recv]).start()

    ki, qi, vi, di = [recv_id() for _ in range(4)]
    ks, qs, vs, ds = to_host_sends = [send_id() for _ in range(4)]

    def slabs():
        to_hosts(k_ref, KU, ki, ks, range(4))
        to_hosts(q_ref, QU, qi, qs, range(4))
        to_hosts(v_ref, VU, vi, vs, range(4))

    for dx in (-1, 1):
        arrived(QA(0, dx), xa[dx])
        if dx == -1:
            part = WA.at[y, ((x + 3) % 4) * 2]
            go(part, all_b, xa[2], xdev(1), f)
        else:
            part = WA.at[y, ((x + 1) % 4) * 2 + 1]
            go(part, all_b, xa[2], xdev(-1), f)
    b_step(1)
    for dx in (-1, 1):
        a_up(0, dx)
        a_down(0, dx)
    slabs()
    arrived(AD1.at[pl.ds(0, 7)], ad1_r)
    AD2[g] = jnp.concatenate([AD1[j] for j in range(8)], axis=0).astype(bf16)
    ad2_s, ad2_r = send_id(), recv_id()
    for j in range(1, 8):
        go(AD2.at[g], ad2_s, ad2_r, at(y, (g + j) % 8), f)

    arrived(QA(0, 2), xa[2])
    a_up(0, 2)
    a_down(0, 2)
    b_step(2)
    a_step(1, 0)
    a_step(1, -1)
    first_row = (y + 8 - c) % 8

    def source_of(slot):
        if slot < 4:
            return jnp.where(shifted_host, at(first_row, slot + 4), at(y, slot))
        return jnp.where(shifted_host, at((first_row + 1) % 8, slot - 4), at(y, slot))

    head_columns = pl.ds(pl.multiple_of(unit_head * 128, 128), 128)

    def from_host(buf, dst_ref, send, recv, slot):
        dest = source_of(slot)
        src, dst = buf.at[slot], dst_ref.at[:, head_columns]
        away = dest != ctx

        @pl.when(away)
        def _():
            go(src, send, recv, dest, f, dst)

        @pl.when(jnp.logical_not(away))
        def _():
            pltpu.make_async_copy(src, dst, rs.at[recv]).start()

    blocks = 1536 // BLOCK

    def two(buf, b):
        return buf[2 * b : 2 * b + 2].reshape(BLOCK, 128)

    def tile(b, kb):
        return b * (b + 1) // 2 + kb

    oh, oi = send_id(), recv_id()

    def forward(b):
        key_at = lax.broadcasted_iota(jnp.int32, (BLOCK, BLOCK), 0)
        query_at = lax.broadcasted_iota(jnp.int32, (BLOCK, BLOCK), 1)
        seen = key_at <= query_at
        query = two(QU, b)
        parts = []
        for kb in range(b + 1):
            part = nt(two(KU, kb), query) * scale
            parts.append(jnp.where(seen, part, masked) if kb == b else part)
        top = jnp.max(parts[0], axis=0, keepdims=True)
        for part in parts[1:]:
            top = jnp.maximum(top, jnp.max(part, axis=0, keepdims=True))
        parts = [jnp.exp(part - top) for part in parts]
        total = jnp.sum(parts[0], axis=0, keepdims=True)
        for part in parts[1:]:
            total = total + jnp.sum(part, axis=0, keepdims=True)
        inverse = 1.0 / total
        out = jnp.zeros((BLOCK, 128), f32)
        for kb in range(b + 1):
            prob = parts[kb] * inverse
            PT[tile(b, kb)] = prob
            out = out + tn(prob.astype(bf16), two(VU, kb))
        OS[2 * b : 2 * b + 2] = out.astype(bf16).reshape(2, 192, 128)
        for s in (2 * b, 2 * b + 1):
            from_host(OS, OB, oh, oi, s)

    def sum_start(n, piece):
        PS[n, f] = piece.astype(bf16)
        send, recv = send_id(), recv_id()
        for j in range(1, 8):
            go(PS.at[n, f], send, recv, ctx, fdev(j))
        return send, recv

    def sum_end(n, pair, factor):
        arrived(PS.at[n, pl.ds(0, 7)], pair[1])
        total = PS[n, 0].astype(f32)
        for j in range(1, 8):
            total = total + PS[n, j].astype(f32)
        return (total * factor).astype(bf16)

    def across_tokens(ranks, low, high):
        return tn(ranks, low)[:64] + tn(ranks, high)[64:]

    b_step(3)
    a_step(1, 1)
    a_step(1, 2)
    x_relay(0)

    below, above, across = fdev(6), fdev(2), fdev(4)
    arrived(GB.at[below], g_low)
    go(GB.at[below, half[0]], gs, g_low_half, ctx, above)
    go(GB.at[below], gs, g_rest, ctx, partner)
    arrived(GB.at[above], g_high)
    go(GB.at[above, half[1]], gs, g_high_half, ctx, below)
    go(GB.at[above], gs, g_rest, ctx, partner)


    @pl.when(is_host)
    def _():
        arrived(KU, ki)
        arrived(QU, qi)
        arrived(VU, vi)
        for kb in range(blocks):
            KT[:, kb * BLOCK : (kb + 1) * BLOCK] = two(KU, kb).astype(f32).T.astype(bf16)
        for b in range(blocks):
            forward(b)

    arrived(PB(-4, 0), yb[-4])
    b_to_x(-4)
    a_step(2, 0)
    a_step(2, -1)
    x_relay(-1)
    x_relay(1)
    arrived(AD2.at[pl.ds(0, 7)], ad2_r)
    adapters = AD2[...].astype(f32).reshape(64, 1152).astype(bf16)
    low = jnp.concatenate([adapters, jnp.zeros_like(adapters)], axis=0)
    high = jnp.concatenate([jnp.zeros_like(adapters), adapters], axis=0)
    down_low, up_low = low[:, :512], low[:, 512:]
    down_high, up_high = high[:, :512], high[:, 512:]
    back0 = sum_start(0, nt(GB[f, 0:96], up_low) + nt(GB[f, 96:192], up_high))

    a_step(2, 1)
    a_step(2, 2)
    x_relay(-2)
    x_relay(2)
    a_step(3, 0)
    a_step(3, -1)
    x_relay(-3)
    x_relay(3)

    a_step(3, 1)
    a_step(3, 2)

    x_relay(-4)
    arrived(OB, oi)
    mid0 = sum_start(1, nt(OB[0:96], down_low) + nt(OB[96:192], down_high))
    arrived(GB.at[across, half[0]], g_low_half)
    go(GB.at[across, half[0]], gs, g_rest, ctx, partner)
    arrived(GB.at[across, half[1]], g_high_half)
    go(GB.at[across, half[1]], gs, g_rest, ctx, partner)

    arrived(GB.at[pl.ds(0, 4)], g_rest)

    def a_part(d):
        yy = row(d)
        return nn(GB[yy], WA[yy].reshape(640, 256))

    total_a = a_part(0)
    for d in (-1, 1, -2, 2, -3, 3):
        total_a = total_a + a_part(d)
    arrived(WB.at[pl.ds(0, 4)], xlast)
    total_b = nn(GB[0], WB[0].reshape(640, 256))
    for yy in range(1, 8):
        total_b = total_b + nn(GB[yy], WB[yy].reshape(640, 256))
    lora_back = sum_end(0, back0, adapter_scale)
    lora_term = jnp.concatenate([nn(lora_back, down_low), nn(lora_back, down_high)], axis=0)
    total_a = total_a + lora_term[:, :256]
    total_b = total_b + lora_term[:, 256:]
    DOB[:, 256:512] = total_b.astype(bf16)
    to_hosts(DOB, DU, di, ds, (2, 3))

    for d, dx in ((-4, 0), (-4, -1), (4, 1), (4, 2)):
        a_arrived(d, dx)
    total_a = total_a + a_part(4)
    DOB[:, 0:256] = total_a.astype(bf16)
    to_hosts(DOB, DU, di, ds, (0, 1))

    gq, gk, gv = [recv_id() for _ in range(3)]
    hq, hk, hv = [send_id() for _ in range(3)]

    def backward(b):
        grad, query = two(DU, b), two(QU, b)
        parts = []
        delta = jnp.zeros((1, BLOCK), f32)
        for kb in range(b + 1):
            part = nt(two(VU, kb), grad)
            delta = delta + jnp.sum(PT[tile(b, kb)] * part, axis=0, keepdims=True)
            parts.append(part)
        turned = jnp.zeros((128, BLOCK), f32)
        for kb in reversed(range(b + 1)):
            span = pl.ds(kb * BLOCK, BLOCK)
            prob = PT[tile(b, kb)]
            pull = (prob * (parts[kb] - delta) * scale).astype(bf16)
            key_part, value_part = nn(pull, query), nn(prob.astype(bf16), grad)
            if b < blocks - 1:
                key_part, value_part = DKA[span] + key_part, DVA[span] + value_part
            if kb == b:
                DKS[2 * b : 2 * b + 2] = key_part.astype(bf16).reshape(2, 192, 128)
                DVS[2 * b : 2 * b + 2] = value_part.astype(bf16).reshape(2, 192, 128)
                for s in (2 * b, 2 * b + 1):
                    from_host(DKS, dk_ref, hk, gk, s)
                    from_host(DVS, dv_ref, hv, gv, s)
            else:
                DKA[span], DVA[span] = key_part, value_part
            turned = turned + nn(KT[:, span], pull)
        DQS[2 * b : 2 * b + 2] = turned.T.astype(bf16).reshape(2, 192, 128)
        for s in (2 * b, 2 * b + 1):
            from_host(DQS, dq_ref, hq, gq, s)

    UPD[:, :, 0:512] = across_tokens(lora_back, OB[0:96], OB[96:192]).reshape(8, 8, 512)
    rs0_s, rs0_r = send_id(), recv_id()
    for j in range(1, 8):
        to = (g + j) % 8
        go(UPD.at[to, :, 0:512], rs0_s, rs0_r, at(y, to), f, R1.at[g, :, 0:512])
    lora_mid = sum_end(1, mid0, adapter_scale)
    up_part = across_tokens(lora_mid, GB[f, 0:96], GB[f, 96:192])
    UPD[:, :, 512:1152] = up_part.reshape(8, 8, 640)
    rs1_s, rs1_r = send_id(), recv_id()
    for j in range(1, 8):
        to = (g + j) % 8
        go(UPD.at[to, :, 512:1152], rs1_s, rs1_r, at(y, to), f, R1.at[g, :, 512:1152])


    @pl.when(is_host)
    def _():
        arrived(DU, di)
        backward(3)

    arrived(R1.at[pl.ds(0, 7), :, 0:512], rs0_r)
    arrived(R1.at[pl.ds(0, 7), :, 512:1152], rs1_r)
    total = UPD[g]
    for j in range(1, 8):
        total = total + R1[(g + j) % 8]
    for j in range(8):
        S2[j] = total[j : j + 1]
    rs2_s, rs2_r = send_id(), recv_id()
    for j in range(1, 8):
        go(S2.at[row(j)], rs2_s, rs2_r, ydev(j), f, R2.at[y])


    @pl.when(is_host)
    def _():
        for b in (2, 1, 0):
            backward(b)

    arrived(R2.at[pl.ds(0, 7)], rs2_r)
    total = S2[y]
    for j in range(1, 8):
        total = total + R2[row(j)]
    dn_ref[...] = total[:, 0:512]
    up_ref[...] = total[:, 512:1152]

    arrived(dq_ref, gq)
    arrived(dk_ref, gk)
    arrived(dv_ref, gv)

    seven = pl.ds(0, 7)
    left(WA.at[0, pl.ds(0, 6)], few)
    left(WB, all_b)
    left(WA.at[seven], all_a)
    left(GB.at[seven], gs)
    left(AD1.at[seven], ad1_s)
    left(AD2.at[seven], ad2_s)
    left(PS.at[0, seven], back0[0])
    left(PS.at[1, seven], mid0[0])
    left(UPD.at[seven, :, 0:512], rs0_s)
    left(UPD.at[seven, :, 512:1152], rs1_s)
    left(S2.at[seven], rs2_s)

    @pl.when(is_host)
    def _():
        for send in to_host_sends:
            left(KU.at[pl.ds(0, 3)], send)
        for send in (oh, hq, hk, hv):
            left(OS.at[seven], send)

    @pl.when(jnp.logical_not(is_host))
    def _():
        for send in to_host_sends:
            left(KU.at[pl.ds(0, 4)], send)

    assert sent[0] <= SENDS and heard[0] <= RECVS, (sent, heard)


def finish_kernel(*refs):
    copies = [pltpu.make_async_copy(refs[n], refs[5 + n], refs[10].at[n]) for n in range(5)]
    for copy in copies:
        copy.start()
    for copy in copies:
        copy.wait()


def on_device(q, k, v, grad, codes, index, table, down, up):
    vmem = pl.BlockSpec(memory_space=pltpu.VMEM)
    tokens, width = q.shape
    out = jax.ShapeDtypeStruct((tokens, width), bf16)
    slabs = pltpu.VMEM((8, 192, 128), bf16)
    results = pl.pallas_call(
        kernel,
        name="block_backward",
        out_shape=(
            out,
            out,
            out,
            jax.ShapeDtypeStruct((1, width), f32),
            jax.ShapeDtypeStruct((1, grad.shape[1]), f32),
        ),
        in_specs=[pl.BlockSpec(memory_space=pl.ANY)] * 9,
        out_specs=[vmem] * 5,
        scratch_shapes=[
            pltpu.VMEM((8, 8, 80, 256), bf16),
            pltpu.VMEM((8, 8, 80, 256), bf16),
            pltpu.VMEM((8, 192, 640), bf16),
            slabs,
            slabs,
            slabs,
            slabs,
            pltpu.VMEM((10, BLOCK, BLOCK), f32),
            pltpu.VMEM((128, 1536), bf16),
            pltpu.VMEM((192, 512), bf16),
            slabs,
            slabs,
            slabs,
            slabs,
            pltpu.VMEM((1536, 128), f32),
            pltpu.VMEM((1536, 128), f32),
            pltpu.VMEM((192, 512), bf16),
            pltpu.VMEM((8, 1, 1152), f32),
            pltpu.VMEM((8, 8, 1152), bf16),
            pltpu.VMEM((2, 8, 96, 128), bf16),
            pltpu.VMEM((8, 8, 1152), f32),
            pltpu.VMEM((8, 8, 1152), f32),
            pltpu.VMEM((8, 1, 1152), f32),
            pltpu.VMEM((8, 1, 1152), f32),
            pltpu.VMEM(codes.shape, jnp.int32),
            pltpu.VMEM(index.shape[::-1], jnp.int32),
            pltpu.VMEM((1, table.shape[0]), f32),
            pltpu.VMEM(down.shape, bf16),
            pltpu.VMEM(up.shape, bf16),
            pltpu.SemaphoreType.DMA((SENDS,)),
            pltpu.SemaphoreType.DMA((RECVS,)),
            pltpu.SemaphoreType.DMA((6,)),
        ],
        compiler_params=pltpu.CompilerParams(
            collective_id=0, has_side_effects=True, vmem_limit_bytes=56 * 1024 * 1024
        ),
    )(codes, index.T, table.reshape(1, -1), down, up, q, k, v, grad)
    return pl.pallas_call(
        finish_kernel,
        name="finish",
        out_shape=tuple(jax.ShapeDtypeStruct(r.shape, r.dtype) for r in results),
        in_specs=[vmem] * 5,
        out_specs=[pl.BlockSpec(memory_space=pl.ANY)] * 5,
        scratch_shapes=[pltpu.SemaphoreType.DMA((5,))],
    )(*results)


def solution(mesh):
    spec = P("ctx", "fsdp")
    return jax.shard_map(
        on_device,
        mesh=mesh,
        in_specs=(spec, spec, spec, spec, spec, spec, P(), spec, spec),
        out_specs=(spec,) * 5,
        check_vma=False,
    )
```

```python
import jax
import jax.numpy as jnp
from jax import lax
from jax.experimental import pallas as pl
from jax.experimental.pallas import tpu as pltpu
from jax.sharding import PartitionSpec as P

HEAD_WIDTH = 128
MESH = pl.DeviceIdType.MESH
BLOCK = 384
nf4_values = (
    -1.0,
    -0.6961928009986877,
    -0.5250730514526367,
    -0.39491748809814453,
    -0.28444138169288635,
    -0.18477343022823334,
    -0.09105003625154495,
    0.0,
    0.07958029955625534,
    0.16093020141124725,
    0.24611230194568634,
    0.33791524171829224,
    0.44070982933044434,
    0.5626170039176941,
    0.7229568362236023,
    1.0,
)
adapter_scale = 0.25
masked = -1e30
f32, bf16 = jnp.float32, jnp.bfloat16
SENDS, RECVS = 24, 76


def nt(a, b):
    return lax.dot_general(a, b, (((1,), (1,)), ((), ())), preferred_element_type=f32)


def tn(a, b):
    return lax.dot_general(a, b, (((0,), (0,)), ((), ())), preferred_element_type=f32)


def nn(a, b):
    return jnp.dot(a, b, preferred_element_type=f32)


def kernel(
    codes_hbm, index_hbm, table_hbm, ad_hbm, au_hbm, q_ref, k_ref, v_ref, g_ref,
    dq_ref, dk_ref, dv_ref, dn_ref, up_ref,
    WA, WB, GB, QU, KU, VU, DU, PT, KT, OB, OS, DQS, DKS, DVS, DKA, DVA, DOB,
    AD1, AD2, PS, UPD, R1, S2, R2, CODES, INDEX, TABLE, DOWN, UP, ss, rs, ls,
):
    ctx = lax.axis_index("ctx")
    f = lax.axis_index("fsdp")
    y, g = ctx // 8, ctx % 8
    x, zl = g // 2, g % 2
    c = f % 2
    partner = f + 1 - 2 * c
    scale = HEAD_WIDTH ** (-0.5)
    shifted_x = 3 * (1 - c)
    shifted_host = x == shifted_x
    is_host = jnp.logical_or(x == 1 + c, shifted_host)
    unit_head = jnp.where(shifted_host, 2, 0) + zl


    sent, heard = [0], [0]

    def send_id():
        sent[0] += 1
        return sent[0] - 1

    def recv_id():
        heard[0] += 1
        return heard[0] - 1

    def remote(src, dst, send, recv, to_ctx, to_f):
        return pltpu.make_async_remote_copy(
            src_ref=src,
            dst_ref=dst,
            send_sem=ss.at[send],
            recv_sem=rs.at[recv],
            device_id={"ctx": to_ctx, "fsdp": to_f},
            device_id_type=MESH,
        )

    def go(src, send, recv, to_ctx, to_f, dst=None):
        remote(src, src if dst is None else dst, send, recv, to_ctx, to_f).start()

    def arrived(dst, recv):
        pltpu.make_async_copy(dst, dst, rs.at[recv]).wait()

    def left(src, send):
        pltpu.make_async_copy(src, src, ss.at[send]).wait()

    def row(dy):
        return (y + dy) % 8

    def at(yy, gg):
        return yy * 8 + gg

    def ydev(dy):
        return at(row(dy), g)

    def xdev(dx):
        return at(y, ((x + dx) % 4) * 2 + zl)

    def fdev(df):
        return (f + df) % 8

    other_row = jnp.where(x < 2, (y + 7) % 8, (y + 1) % 8)
    other_g = jnp.where(x < 2, 4, 0)

    barrier = pltpu.get_barrier_semaphore()
    peers = [(at(y, (g + j) % 8), f) for j in range(1, 8)]
    peers += [(ydev(j), f) for j in range(1, 8)]
    peers += [(ctx, fdev(j)) for j in range(1, 8)]
    peers += [(at(other_row, other_g + j), f) for j in range(4)]
    for to_ctx, to_f in peers:
        pl.semaphore_signal(
            barrier, inc=1, device_id={"ctx": to_ctx, "fsdp": to_f}, device_id_type=MESH
        )
    own_grad = pltpu.make_async_copy(g_ref, GB.at[f], ls.at[0])
    loads = [
        pltpu.make_async_copy(src, dst, ls.at[n + 1])
        for n, (src, dst) in enumerate(
            (
                (codes_hbm, CODES),
                (index_hbm, INDEX),
                (table_hbm, TABLE),
                (ad_hbm, DOWN),
                (au_hbm, UP),
            )
        )
    ]
    for copy in loads:
        copy.start()
    own_grad.start()
    for copy in loads:
        copy.wait()

    codes = CODES[...]
    values = jnp.zeros(codes.shape, f32)
    for level in range(16):
        values = jnp.where(codes == level, nf4_values[level], values)
    table = TABLE[...]
    index = jnp.concatenate([INDEX[...].astype(f32), jnp.zeros((8, 48), f32)], axis=1)
    index = index.T[: codes.shape[0]].astype(jnp.int32)
    level_at = lax.broadcasted_iota(jnp.int32, (codes.shape[0], table.shape[1]), 1)
    block_at = lax.broadcasted_iota(jnp.int32, codes.shape, 1) // 64
    scales = jnp.zeros(codes.shape, f32)
    for block in range(8):
        picked = jnp.where(index[:, block : block + 1] == level_at, table, 0.0)
        picked = jnp.sum(picked, axis=1, keepdims=True)
        scales = jnp.where(block_at == block, picked, scales)
    weight = (values * scales).astype(bf16)
    WA[y, g] = weight[:, :256]
    WB[y, g] = weight[:, 256:]
    AD1[y] = jnp.concatenate([DOWN[...].astype(f32), UP[...].astype(f32)], axis=1)
    pl.semaphore_wait(barrier, len(peers))

    pair = ctx + 1 - 2 * zl
    first, few = recv_id(), send_id()
    go(WA.at[y, g], few, first, pair, f)
    go(WB.at[y, g], few, first, pair, f)

    ad1_s, ad1_r = send_id(), recv_id()
    for j in range(1, 8):
        go(AD1.at[y], ad1_s, ad1_r, ydev(j), f)

    def PB(dy, dx):
        return WB.at[row(dy), pl.ds(((x + dx) % 4) * 2, 2)]

    def QA(dy, dx):
        return WA.at[row(dy), pl.ds(((x + dx) % 4) * 2, 2)]

    up_relay = (-1, 0, 1)
    yb = {d: recv_id() for d in (-4, -3, -2, -1, 1, 2, 3)}
    xlast = recv_id()
    xb = {}
    for d in range(-4, 4):
        xb[(-1, d)] = recv_id() if d in up_relay else xlast
        xb[(1, d)] = xlast if d in up_relay else recv_id()
    all_b, all_a = send_id(), send_id()

    def b_to_x(d):
        go(PB(d, 0), all_b, xb[(-1, d)], xdev(1), f)
        go(PB(d, 0), all_b, xb[(1, d)], xdev(-1), f)

    def b_up(d):
        go(PB(d, 0), all_b, yb[d - 1], ydev(1), f)

    def b_down(d):
        go(PB(d, 0), all_b, yb[d + 1], ydev(-1), f)

    def x_relay(d):
        side = -1 if d in up_relay else 1
        arrived(PB(d, side), xb[(side, d)])
        go(PB(d, side), all_b, xlast, xdev(-side), f)

    around = (0, -1, 1, 2)
    ya = {(d, dx): recv_id() for d in (-3, -2, -1, 1, 2, 3) for dx in around}
    for d, dx in ((-4, 0), (-4, -1), (4, 1), (4, 2)):
        ya[(d, dx)] = recv_id()

    def a_up(d, dx):
        go(QA(d, dx), all_a, ya[(d - 1, dx)], ydev(1), f)

    def a_down(d, dx):
        go(QA(d, dx), all_a, ya[(d + 1, dx)], ydev(-1), f)

    def a_arrived(d, dx):
        arrived(QA(d, dx), ya[(d, dx)])

    def a_step(d, dx):
        a_arrived(-d, dx)
        if d < 3 or dx in (0, -1):
            a_up(-d, dx)
        a_arrived(d, dx)
        if d < 3 or dx in (1, 2):
            a_down(d, dx)

    def b_step(d):
        arrived(PB(-d, 0), yb[-d])
        b_up(-d)
        b_to_x(-d)
        arrived(PB(d, 0), yb[d])
        if d < 3:
            b_down(d)
        b_to_x(d)

    xa = {dx: recv_id() for dx in (-1, 1, 2)}

    def spread(z):
        block_a, block_b = WA.at[y, 2 * x + z], WB.at[y, 2 * x + z]
        for up in (1, -1):
            go(block_b, all_b, yb[-up], ydev(up), f)
            go(block_a, few, xa[-up], xdev(up), f)
            go(block_b, all_b, xb[(-up, 0)], xdev(up), f)
            go(block_a, all_a, ya[(-up, 0)], ydev(up), f)

    spread(zl)
    arrived(WA.at[0, pl.ds(0, 2)], first)
    spread(1 - zl)

    half = [pl.ds(0, 96), pl.ds(96, 96)]
    gs = send_id()
    g_own, g_low, g_high, g_low_half, g_high_half, g_rest = [recv_id() for _ in range(6)]
    own_grad.wait()
    go(GB.at[f], gs, g_low, ctx, fdev(2))
    go(GB.at[f], gs, g_high, ctx, fdev(6))
    go(GB.at[f], gs, g_rest, ctx, partner)

    def slab_of(head):
        return g if head < 2 else (g + 4) % 8

    def host_of(head):
        if head < 2:
            return at(y, (1 + c) * 2 + head)
        first_row = jnp.where(x < 2, (y + 7) % 8, y)
        return at((first_row + c) % 8, shifted_x * 2 + head - 2)

    to_host_sends = []

    def to_hosts(src_ref, dst_buf, recvs, send, heads):
        for head in heads:
            dest = host_of(head)
            slot = slab_of(head)
            src = src_ref.at[:, head * 128 : (head + 1) * 128]
            dst = dst_buf.at[slot]
            recv = recvs[0] + slot // 2 if len(recvs) > 1 else recvs[0]
            away = dest != ctx

            @pl.when(away)
            def _():
                go(src, send, recv, dest, f, dst)

            @pl.when(jnp.logical_not(away))
            def _():
                pltpu.make_async_copy(src, dst, rs.at[recv]).start()

    ki, qi, vi = [recv_id() for _ in range(3)]
    di = [recv_id() for _ in range(4)]
    ks, qs, vs, ds = to_host_sends = [send_id() for _ in range(4)]

    def slabs():
        to_hosts(k_ref, KU, [ki], ks, range(4))
        to_hosts(q_ref, QU, [qi], qs, range(4))
        to_hosts(v_ref, VU, [vi], vs, range(4))

    for dx in (-1, 1):
        arrived(QA(0, dx), xa[dx])
        if dx == -1:
            part = WA.at[y, ((x + 3) % 4) * 2]
            go(part, all_b, xa[2], xdev(1), f)
        else:
            part = WA.at[y, ((x + 1) % 4) * 2 + 1]
            go(part, all_b, xa[2], xdev(-1), f)
    b_step(1)
    for dx in (-1, 1):
        a_up(0, dx)
        a_down(0, dx)
    slabs()
    arrived(AD1.at[pl.ds(0, 7)], ad1_r)
    AD2[g] = jnp.concatenate([AD1[j] for j in range(8)], axis=0).astype(bf16)
    ad2_s, ad2_r = send_id(), recv_id()
    for j in range(1, 8):
        go(AD2.at[g], ad2_s, ad2_r, at(y, (g + j) % 8), f)

    arrived(QA(0, 2), xa[2])
    a_up(0, 2)
    a_down(0, 2)
    b_step(2)
    a_step(1, 0)
    a_step(1, -1)
    first_row = (y + 8 - c) % 8

    def source_of(slot):
        if slot < 4:
            return jnp.where(shifted_host, at(first_row, slot + 4), at(y, slot))
        return jnp.where(shifted_host, at((first_row + 1) % 8, slot - 4), at(y, slot))

    head_columns = pl.ds(pl.multiple_of(unit_head * 128, 128), 128)

    def from_host(buf, dst_ref, send, recv, slot):
        dest = source_of(slot)
        src, dst = buf.at[slot], dst_ref.at[:, head_columns]
        away = dest != ctx

        @pl.when(away)
        def _():
            go(src, send, recv, dest, f, dst)

        @pl.when(jnp.logical_not(away))
        def _():
            pltpu.make_async_copy(src, dst, rs.at[recv]).start()

    blocks = 1536 // BLOCK

    def two(buf, b):
        return buf[2 * b : 2 * b + 2].reshape(BLOCK, 128)

    def tile(b, kb):
        return b * (b + 1) // 2 + kb

    oh, oi = send_id(), recv_id()

    def forward(b):
        key_at = lax.broadcasted_iota(jnp.int32, (BLOCK, BLOCK), 0)
        query_at = lax.broadcasted_iota(jnp.int32, (BLOCK, BLOCK), 1)
        seen = key_at <= query_at
        query = two(QU, b)
        parts = []
        for kb in range(b + 1):
            part = nt(two(KU, kb), query) * scale
            parts.append(jnp.where(seen, part, masked) if kb == b else part)
        top = jnp.max(parts[0], axis=0, keepdims=True)
        for part in parts[1:]:
            top = jnp.maximum(top, jnp.max(part, axis=0, keepdims=True))
        parts = [jnp.exp(part - top) for part in parts]
        total = jnp.sum(parts[0], axis=0, keepdims=True)
        for part in parts[1:]:
            total = total + jnp.sum(part, axis=0, keepdims=True)
        inverse = 1.0 / total
        out = jnp.zeros((BLOCK, 128), f32)
        for kb in range(b + 1):
            prob = parts[kb] * inverse
            PT[tile(b, kb)] = prob
            out = out + tn(prob.astype(bf16), two(VU, kb))
        OS[2 * b : 2 * b + 2] = out.astype(bf16).reshape(2, 192, 128)
        for s in (2 * b, 2 * b + 1):
            from_host(OS, OB, oh, oi, s)

    def sum_start(n, piece):
        PS[n, f] = piece.astype(bf16)
        send, recv = send_id(), recv_id()
        for j in range(1, 8):
            go(PS.at[n, f], send, recv, ctx, fdev(j))
        return send, recv

    def sum_end(n, pair, factor):
        arrived(PS.at[n, pl.ds(0, 7)], pair[1])
        total = PS[n, 0].astype(f32)
        for j in range(1, 8):
            total = total + PS[n, j].astype(f32)
        return (total * factor).astype(bf16)

    def across_tokens(ranks, low, high):
        return tn(ranks, low)[:64] + tn(ranks, high)[64:]

    b_step(3)
    a_step(1, 1)
    a_step(1, 2)
    x_relay(0)

    below, above, across = fdev(6), fdev(2), fdev(4)
    arrived(GB.at[below], g_low)
    go(GB.at[below, half[0]], gs, g_low_half, ctx, above)
    go(GB.at[below], gs, g_rest, ctx, partner)
    arrived(GB.at[above], g_high)
    go(GB.at[above, half[1]], gs, g_high_half, ctx, below)
    go(GB.at[above], gs, g_rest, ctx, partner)


    @pl.when(is_host)
    def _():
        arrived(KU, ki)
        arrived(QU, qi)
        arrived(VU, vi)
        for kb in range(blocks):
            KT[:, kb * BLOCK : (kb + 1) * BLOCK] = two(KU, kb).astype(f32).T.astype(bf16)
        for b in range(blocks):
            forward(b)

    arrived(PB(-4, 0), yb[-4])
    b_to_x(-4)
    a_step(2, 0)
    a_step(2, -1)
    x_relay(-1)
    x_relay(1)
    arrived(AD2.at[pl.ds(0, 7)], ad2_r)
    adapters = AD2[...].astype(f32).reshape(64, 1152).astype(bf16)
    low = jnp.concatenate([adapters, jnp.zeros_like(adapters)], axis=0)
    high = jnp.concatenate([jnp.zeros_like(adapters), adapters], axis=0)
    down_low, up_low = low[:, :512], low[:, 512:]
    down_high, up_high = high[:, :512], high[:, 512:]
    back0 = sum_start(0, nt(GB[f, 0:96], up_low) + nt(GB[f, 96:192], up_high))

    a_step(2, 1)
    a_step(2, 2)
    x_relay(-2)
    x_relay(2)
    a_step(3, 0)
    a_step(3, -1)
    x_relay(-3)
    x_relay(3)

    arrived(GB.at[across, half[0]], g_low_half)
    go(GB.at[across, half[0]], gs, g_rest, ctx, partner)
    arrived(GB.at[across, half[1]], g_high_half)
    go(GB.at[across, half[1]], gs, g_rest, ctx, partner)

    a_step(3, 1)
    a_step(3, 2)

    x_relay(-4)
    arrived(OB, oi)
    mid0 = sum_start(1, nt(OB[0:96], down_low) + nt(OB[96:192], down_high))
    arrived(GB.at[pl.ds(0, 4)], g_rest)

    def a_part(d):
        yy = row(d)
        return nn(GB[yy], WA[yy].reshape(640, 256))

    total_a = a_part(0)
    for d in (-1, 1, -2, 2, -3, 3):
        total_a = total_a + a_part(d)
    arrived(WB.at[pl.ds(0, 4)], xlast)
    total_b = nn(GB[0], WB[0].reshape(640, 256))
    for yy in range(1, 8):
        total_b = total_b + nn(GB[yy], WB[yy].reshape(640, 256))
    lora_back = sum_end(0, back0, adapter_scale)
    lora_term = jnp.concatenate([nn(lora_back, down_low), nn(lora_back, down_high)], axis=0)
    total_a = total_a + lora_term[:, :256]
    total_b = total_b + lora_term[:, 256:]
    DOB[:, 256:512] = total_b.astype(bf16)
    to_hosts(DOB, DU, di, ds, (2, 3))

    for d, dx in ((-4, 0), (-4, -1), (4, 1), (4, 2)):
        a_arrived(d, dx)
    total_a = total_a + a_part(4)
    DOB[:, 0:256] = total_a.astype(bf16)
    to_hosts(DOB, DU, di, ds, (0, 1))

    gq, gk, gv = [recv_id() for _ in range(3)]
    hq, hk, hv = [send_id() for _ in range(3)]

    def backward(b):
        arrived(DU.at[pl.ds(2 * b, 2)], di[b])
        grad, query = two(DU, b), two(QU, b)
        parts = []
        delta = jnp.zeros((1, BLOCK), f32)
        for kb in range(b + 1):
            part = nt(two(VU, kb), grad)
            delta = delta + jnp.sum(PT[tile(b, kb)] * part, axis=0, keepdims=True)
            parts.append(part)
        turned = jnp.zeros((128, BLOCK), f32)
        for kb in reversed(range(b + 1)):
            span = pl.ds(kb * BLOCK, BLOCK)
            prob = PT[tile(b, kb)]
            pull = (prob * (parts[kb] - delta) * scale).astype(bf16)
            key_part, value_part = nn(pull, query), nn(prob.astype(bf16), grad)
            if b < blocks - 1:
                key_part, value_part = DKA[span] + key_part, DVA[span] + value_part
            if kb == b:
                DKS[2 * b : 2 * b + 2] = key_part.astype(bf16).reshape(2, 192, 128)
                DVS[2 * b : 2 * b + 2] = value_part.astype(bf16).reshape(2, 192, 128)
                for s in (2 * b, 2 * b + 1):
                    from_host(DKS, dk_ref, hk, gk, s)
                    from_host(DVS, dv_ref, hv, gv, s)
            else:
                DKA[span], DVA[span] = key_part, value_part
            turned = turned + nn(KT[:, span], pull)
        DQS[2 * b : 2 * b + 2] = turned.T.astype(bf16).reshape(2, 192, 128)
        for s in (2 * b, 2 * b + 1):
            from_host(DQS, dq_ref, hq, gq, s)

    UPD[:, :, 0:512] = across_tokens(lora_back, OB[0:96], OB[96:192]).reshape(8, 8, 512)
    rs0_s, rs0_r = send_id(), recv_id()
    for j in range(1, 8):
        to = (g + j) % 8
        go(UPD.at[to, :, 0:512], rs0_s, rs0_r, at(y, to), f, R1.at[g, :, 0:512])
    lora_mid = sum_end(1, mid0, adapter_scale)
    up_part = across_tokens(lora_mid, GB[f, 0:96], GB[f, 96:192])
    UPD[:, :, 512:1152] = up_part.reshape(8, 8, 640)
    rs1_s, rs1_r = send_id(), recv_id()
    for j in range(1, 8):
        to = (g + j) % 8
        go(UPD.at[to, :, 512:1152], rs1_s, rs1_r, at(y, to), f, R1.at[g, :, 512:1152])


    @pl.when(is_host)
    def _():
        backward(3)

    arrived(R1.at[pl.ds(0, 7), :, 0:512], rs0_r)
    arrived(R1.at[pl.ds(0, 7), :, 512:1152], rs1_r)
    total = UPD[g]
    for j in range(1, 8):
        total = total + R1[(g + j) % 8]
    for j in range(8):
        S2[j] = total[j : j + 1]
    rs2_s, rs2_r = send_id(), recv_id()
    for j in range(1, 8):
        go(S2.at[row(j)], rs2_s, rs2_r, ydev(j), f, R2.at[y])


    @pl.when(is_host)
    def _():
        for b in (2, 1, 0):
            backward(b)

    arrived(R2.at[pl.ds(0, 7)], rs2_r)
    total = S2[y]
    for j in range(1, 8):
        total = total + R2[row(j)]
    dn_ref[...] = total[:, 0:512]
    up_ref[...] = total[:, 512:1152]

    arrived(dq_ref, gq)
    arrived(dk_ref, gk)
    arrived(dv_ref, gv)

    seven = pl.ds(0, 7)
    left(WA.at[0, pl.ds(0, 6)], few)
    left(WB, all_b)
    left(WA.at[seven], all_a)
    left(GB.at[seven], gs)
    left(AD1.at[seven], ad1_s)
    left(AD2.at[seven], ad2_s)
    left(PS.at[0, seven], back0[0])
    left(PS.at[1, seven], mid0[0])
    left(UPD.at[seven, :, 0:512], rs0_s)
    left(UPD.at[seven, :, 512:1152], rs1_s)
    left(S2.at[seven], rs2_s)

    @pl.when(is_host)
    def _():
        for send in to_host_sends:
            left(KU.at[pl.ds(0, 3)], send)
        for send in (oh, hq, hk, hv):
            left(OS.at[seven], send)

    @pl.when(jnp.logical_not(is_host))
    def _():
        for send in to_host_sends:
            left(KU.at[pl.ds(0, 4)], send)

    assert sent[0] <= SENDS and heard[0] <= RECVS, (sent, heard)


def finish_kernel(*refs):
    copies = [pltpu.make_async_copy(refs[n], refs[5 + n], refs[10].at[n]) for n in range(5)]
    for copy in copies:
        copy.start()
    for copy in copies:
        copy.wait()


def on_device(q, k, v, grad, codes, index, table, down, up):
    vmem = pl.BlockSpec(memory_space=pltpu.VMEM)
    tokens, width = q.shape
    out = jax.ShapeDtypeStruct((tokens, width), bf16)
    slabs = pltpu.VMEM((8, 192, 128), bf16)
    results = pl.pallas_call(
        kernel,
        name="block_backward",
        out_shape=(
            out,
            out,
            out,
            jax.ShapeDtypeStruct((1, width), f32),
            jax.ShapeDtypeStruct((1, grad.shape[1]), f32),
        ),
        in_specs=[pl.BlockSpec(memory_space=pl.ANY)] * 9,
        out_specs=[vmem] * 5,
        scratch_shapes=[
            pltpu.VMEM((8, 8, 80, 256), bf16),
            pltpu.VMEM((8, 8, 80, 256), bf16),
            pltpu.VMEM((8, 192, 640), bf16),
            slabs,
            slabs,
            slabs,
            slabs,
            pltpu.VMEM((10, BLOCK, BLOCK), f32),
            pltpu.VMEM((128, 1536), bf16),
            pltpu.VMEM((192, 512), bf16),
            slabs,
            slabs,
            slabs,
            slabs,
            pltpu.VMEM((1536, 128), f32),
            pltpu.VMEM((1536, 128), f32),
            pltpu.VMEM((192, 512), bf16),
            pltpu.VMEM((8, 1, 1152), f32),
            pltpu.VMEM((8, 8, 1152), bf16),
            pltpu.VMEM((2, 8, 96, 128), bf16),
            pltpu.VMEM((8, 8, 1152), f32),
            pltpu.VMEM((8, 8, 1152), f32),
            pltpu.VMEM((8, 1, 1152), f32),
            pltpu.VMEM((8, 1, 1152), f32),
            pltpu.VMEM(codes.shape, jnp.int32),
            pltpu.VMEM(index.shape[::-1], jnp.int32),
            pltpu.VMEM((1, table.shape[0]), f32),
            pltpu.VMEM(down.shape, bf16),
            pltpu.VMEM(up.shape, bf16),
            pltpu.SemaphoreType.DMA((SENDS,)),
            pltpu.SemaphoreType.DMA((RECVS,)),
            pltpu.SemaphoreType.DMA((6,)),
        ],
        compiler_params=pltpu.CompilerParams(
            collective_id=0, has_side_effects=True, vmem_limit_bytes=56 * 1024 * 1024
        ),
    )(codes, index.T, table.reshape(1, -1), down, up, q, k, v, grad)
    return pl.pallas_call(
        finish_kernel,
        name="finish",
        out_shape=tuple(jax.ShapeDtypeStruct(r.shape, r.dtype) for r in results),
        in_specs=[vmem] * 5,
        out_specs=[pl.BlockSpec(memory_space=pl.ANY)] * 5,
        scratch_shapes=[pltpu.SemaphoreType.DMA((5,))],
    )(*results)


def solution(mesh):
    spec = P("ctx", "fsdp")
    return jax.shard_map(
        on_device,
        mesh=mesh,
        in_specs=(spec, spec, spec, spec, spec, spec, P(), spec, spec),
        out_specs=(spec,) * 5,
        check_vma=False,
    )
```
